256 devices in a mesh: grid: 2 (over x_hi), prow: 4 (over x_lo, core), pcol: 32 (over z, y).
Axes of the slice: x: 4 (x_hi: 2, x_lo: 2; x = x_hi * 2 + x_lo), y: 4, z: 8, core: 2. Of those that a mesh axis runs over, the one named last changes fastest.
Arguments:
- sub_rhs: float32 [8, 3, 64, 3072], P('grid', None, None, 'prow'), may hold values from -6 to 6
- root_rhs: float32 [64, 3072], P(None, 'prow'), may hold values from -6 to 6
- diag_inverse: bfloat16 [3, 3072, 24576], P(None, 'prow', ('grid', 'pcol'))
- root_inverse: bfloat16 [3072, 3072], P('prow', 'grid')
- inner_factor: bfloat16 [3, 24576, 3072], P(None, ('grid', 'pcol'), 'prow'), may hold values from -0.078125 to 0.078125
- inner_mask: int32 [3, 192, 24], P(None, ('grid', 'pcol')), may hold values 0 or 1
- root_factor: bfloat16 [3, 24576, 3072], P(None, ('grid', 'pcol'), 'prow'), may hold values from -0.078125 to 0.078125
- root_mask: int32 [3, 192, 24], P(None, ('grid', 'pcol')), may hold values 0 or 1
Outputs:
- sub_solution: float32 [3, 64, 24576], P(None, None, ('grid', 'pcol'))
- root_solution: float32 [64, 3072], P(None, 'grid')
The draws below stay inside these ranges and needn't reach their ends.
Inputs may be any that keep to these rules, and one draw needn't show every extreme that they name: `inner_mask`: 1 keeps a tile of 128 x 128 entries, 0 makes it zero. `root_mask`: 1 keeps a tile of 128 x 128 entries, 0 makes it zero.
All inputs are finite; a program needn't handle non-finite values. No bound on the sum of `inner_mask` or of `root_mask` on one device may be relied on, other than what follows from the above.
Results may differ from the reference program's by a relative error of at most 0.0065.
Values sent between devices are 32-bit elements; how exact they have to be, the bound alone decides.
No kernel may reach another device: no remote copies, remote signals or barrier semaphores. Data moves between devices by JAX's collectives and lax.ppermute only.
A program may use at most 64 MiB of HBM per device.

```python
import jax
import jax.numpy as jnp

NS = 3072
NRHS = 64
LEVELS = 3
TILE = 128
SUBTREES = 8
PAIRS = 3
TB = 24


def spread_of(key, shape):
    return jax.random.normal(key, shape, jnp.float32) * (0.4 / NS ** 0.5)


def draw_diag_inverse(key, part):
    base = jax.random.fold_in(key, 11)
    first, second = jax.random.split(base)
    diagonal = jax.random.uniform(first, (LEVELS, SUBTREES, NS), jnp.float32, 1.0, 2.0)
    spread = spread_of(second, (LEVELS, NS, SUBTREES * NS))
    identity = jnp.eye(NS, dtype=jnp.float32)
    placed = identity[None, :, None, :] * diagonal[:, None, :, :]
    whole = spread + placed.reshape(LEVELS, NS, SUBTREES * NS)
    return whole.astype(jnp.bfloat16)


def draw_root_inverse(key, part):
    base = jax.random.fold_in(key, 23)
    first, second = jax.random.split(base)
    diagonal = jax.random.uniform(first, (NS,), jnp.float32, 1.0, 2.0)
    spread = spread_of(second, (NS, NS))
    whole = spread + diagonal[:, None] * jnp.eye(NS, dtype=jnp.float32)
    return whole.astype(jnp.bfloat16)


def place_ends(entries, stream_key, smallest, top_value):
    place = [jax.random.randint(jax.random.fold_in(stream_key, axis), (), 0, length) for axis, length in enumerate(entries.shape)]
    widest = entries.shape.index(max(entries.shape))
    neighbour = place[:widest] + [(place[widest] + 1) % entries.shape[widest]] + place[widest + 1:]
    return entries.at[tuple(place)].set(smallest).at[tuple(neighbour)].set(top_value)


def levels(stream_key, extent, cuts, low, largest):
    gain = 1.0
    for dim, shards_of in cuts:
        draws = jax.random.uniform(jax.random.fold_in(jax.random.fold_in(stream_key, 6), dim), (shards_of,), jnp.float32, low / len(cuts), largest / len(cuts))
        gain = gain * jnp.repeat(jnp.exp(draws), extent[dim] // shards_of).reshape((-1,) + (1,) * (len(extent) - 1 - dim))
    return gain


def normal_values(stream_key, dims, width, most, pieces=(), kind=jnp.bfloat16):
    array = jax.random.normal(stream_key, dims, jnp.float32) * width
    if len(pieces) > 0:
        array = levels(stream_key, dims, pieces, -0.22, 0.18) * array
    return jnp.clip(array, min=-most, max=most).astype(kind)


def setup_inputs(seed: int = 0) -> dict:
    streams_of = jax.random.split(jax.random.key(seed), 9)
    sub_rhs = normal_values(streams_of[0], (SUBTREES, LEVELS, NRHS, NS), 1.0, 6.0, ((0, 2), (3, 4)), jnp.float32)
    root_rhs = normal_values(streams_of[1], (NRHS, NS), 1.0, 6.0, ((1, 4),), jnp.float32)
    diag_inverse = draw_diag_inverse(jax.random.fold_in(streams_of[8], 71), 0)
    root_inverse = draw_root_inverse(jax.random.fold_in(streams_of[8], 71), 0)
    inner_factor = normal_values(streams_of[4], (PAIRS, SUBTREES * NS, NS), (2 * NS) ** -0.5, 0.078125, ((1, 64), (2, 4)))
    inner_mask = place_ends((jax.random.randint(streams_of[5], (PAIRS, SUBTREES * TB, TB), 0, 4) < 3).astype(jnp.int32), jax.random.fold_in(streams_of[5], 1), 0, 1)
    root_factor = normal_values(streams_of[6], (LEVELS, SUBTREES * NS, NS), (2 * NS) ** -0.5, 0.078125, ((1, 64), (2, 4)))
    root_mask = place_ends((jax.random.randint(streams_of[7], (LEVELS, SUBTREES * TB, TB), 0, 4) < 3).astype(jnp.int32), jax.random.fold_in(streams_of[7], 1), 0, 1)
    return dict(sub_rhs=sub_rhs, root_rhs=root_rhs, diag_inverse=diag_inverse, root_inverse=root_inverse, inner_factor=inner_factor, inner_mask=inner_mask, root_factor=root_factor, root_mask=root_mask)


def expand(mask):
    wide = jnp.repeat(jnp.repeat(mask, TILE, axis=0), TILE, axis=1)
    return wide.astype(jnp.bfloat16)


def reference(sub_rhs, root_rhs, diag_inverse, root_inverse, inner_factor, inner_mask, root_factor, root_mask):
    root_update = jnp.zeros((NRHS, NS), jnp.float32)
    results = []
    for tree in range(SUBTREES):
        first_row = tree * NS
        first_tile = tree * TB
        kept = []
        levels_out = []
        pair = 0
        for level in range(LEVELS):
            update = jnp.zeros((NRHS, NS), jnp.float32)
            for source in range(level):
                factor = inner_factor[pair, first_row:first_row + NS]
                block = factor * expand(inner_mask[pair, first_tile:first_tile + TB])
                update = update + jnp.dot(kept[source], block, preferred_element_type=jnp.float32)
                pair += 1
            residual = (sub_rhs[tree, level] - update).astype(jnp.bfloat16)
            inverse = diag_inverse[level, :, first_row:first_row + NS]
            solved = jnp.dot(residual, inverse, preferred_element_type=jnp.float32)
            levels_out.append(solved)
            kept.append(solved.astype(jnp.bfloat16))
        for source in range(LEVELS):
            factor = root_factor[source, first_row:first_row + NS]
            block = factor * expand(root_mask[source, first_tile:first_tile + TB])
            root_update = root_update + jnp.dot(kept[source], block, preferred_element_type=jnp.float32)
        results.append(jnp.stack(levels_out))
    root_residual = (root_rhs - root_update).astype(jnp.bfloat16)
    root_solution = jnp.dot(root_residual, root_inverse, preferred_element_type=jnp.float32)
    return jnp.concatenate(results, axis=2), root_solution
```

```python
import jax
import jax.numpy as jnp
from jax import lax
from jax.sharding import Mesh
from jax.sharding import PartitionSpec as P

LEVELS = 3
TILE = 128
PROW = ("xl", "core")
OWN = ("zl", "y")
TREES = ("grid", "zt")


def partner(shard, axis, bit=1):
    return lax.ppermute(shard, axis, [(i, i ^ bit) for i in range(lax.axis_size(axis))])


def to_everyone(shard, axis):
    count = lax.axis_size(axis)
    return lax.all_to_all(
        jnp.broadcast_to(shard[None], (count, *shard.shape)), axis, 0, 0, tiled=True
    )


def prow_sum(partial_sum):
    pair = partial_sum + partner(partial_sum, "core")
    return pair + partner(pair, "xl")


def owner_sum(partial_sum):
    total = partial_sum + partner(partial_sum, "zl")
    total = total + partner(total, "y", 1)
    return total + partner(total, "y", 2)


def product(left, right):
    return jnp.dot(left, right, preferred_element_type=jnp.float32)


def selector(positions, count):
    return (positions[:, None] // TILE == jnp.arange(count)[None, :]).astype(jnp.float32)


def masked(factor, mask, row_select, col_select):
    expanded = jnp.dot(jnp.dot(row_select, mask.astype(jnp.float32)), col_select.T)
    return factor * expanded.astype(jnp.bfloat16)


def shards(
    sub_rhs, root_rhs, diag_inverse, root_inverse, inner_factor, inner_mask, root_factor, root_mask
):
    rows_here = inner_factor.shape[1]
    out_cols = inner_factor.shape[2]
    rhs_count = root_rhs.shape[0]
    col_positions = lax.axis_index(PROW) * out_cols + jnp.arange(out_cols)
    row_select = selector(jnp.arange(rows_here), inner_mask.shape[1])
    col_select = selector(col_positions, inner_mask.shape[2])
    own_rhs = lax.dynamic_index_in_dim(sub_rhs, lax.axis_index("zt"), 0, keepdims=False)

    kept = []
    solved_all = []
    pair = 0
    for level in range(LEVELS):
        residual = own_rhs[level]
        if level > 0:
            local_update = jnp.zeros(residual.shape, jnp.float32)
            for source in range(level):
                tile = masked(inner_factor[pair], inner_mask[pair], row_select, col_select)
                local_update = local_update + product(kept[source], tile)
                pair += 1
            residual = residual - owner_sum(local_update)
        solved = prow_sum(product(residual.astype(jnp.bfloat16), diag_inverse[level]))
        solved_all.append(solved)
        kept.append(solved.astype(jnp.bfloat16))

    root_local = jnp.zeros(root_rhs.shape, jnp.float32)
    for source in range(LEVELS):
        tile = masked(root_factor[source], root_mask[source], row_select, col_select)
        root_local = root_local + product(kept[source], tile)

    owners = lax.axis_size(OWN)
    few = rhs_count // owners
    own_rows = lax.all_to_all(
        root_local.reshape(owners, few, out_cols), OWN, 0, 0, tiled=True
    ).sum(axis=0)
    root_update = to_everyone(own_rows, TREES).sum(axis=0)
    rhs_rows = lax.dynamic_slice_in_dim(root_rhs, lax.axis_index(OWN) * few, few, 0)
    root_residual = (rhs_rows - root_update).astype(jnp.bfloat16)
    part = product(root_residual, root_inverse)
    half = part.shape[1] // 2
    first = lax.axis_index("core") == 0
    low, high = part[:, :half], part[:, half:]
    mine = jnp.where(first, low, high) + partner(jnp.where(first, high, low), "core")
    mine = mine + partner(mine, "xl")
    columns = to_everyone(mine, OWN).reshape(rhs_count, half)
    others = partner(columns, "core")
    root_solution = jnp.concatenate(
        [jnp.where(first, columns, others), jnp.where(first, others, columns)], axis=1
    )
    return (jnp.stack(solved_all), root_solution)


def solution(mesh):
    prow, pcol = mesh.shape["prow"], mesh.shape["pcol"]
    cores, y = 2, 4
    trees = 8 // mesh.shape["grid"]
    fine = Mesh(
        mesh.devices.reshape(
            mesh.shape["grid"], prow // cores, cores, trees, pcol // (trees * y), y
        ),
        ("grid", "xl", "core", "zt", "zl", "y"),
    )
    columns = ("grid", "zt", "zl", "y")
    return jax.shard_map(
        shards,
        mesh=fine,
        in_specs=(
            P("grid", None, None, PROW),
            P(None, PROW),
            P(None, PROW, columns),
            P(PROW, "grid"),
            P(None, columns, PROW),
            P(None, columns, None),
            P(None, columns, PROW),
            P(None, columns, None),
        ),
        out_specs=(P(None, None, columns), P(None, "grid")),
        check_vma=False,
    )
```

```python
import jax
import jax.numpy as jnp
from jax import lax
from jax.experimental import pallas as pl
from jax.experimental.pallas import tpu as pltpu
from jax.sharding import Mesh
from jax.sharding import PartitionSpec as P

LEVELS = 3
TILE = 128
PROW = ("xl", "core")
OWN = ("zl", "y")
SCOPED_BYTES = 4 << 20
F32 = jnp.float32
BF16 = jnp.bfloat16

ON_CHIP = pl.BlockSpec(memory_space=pltpu.VMEM)
SCALARS = pl.BlockSpec(memory_space=pltpu.SMEM)
IN_PLACE = pl.BlockSpec(memory_space=pltpu.HBM)


def partner(shard, axis, bit=1):
    return lax.ppermute(shard, axis, [(i, i ^ bit) for i in range(lax.axis_size(axis))])


def to_everyone(shard, axis):
    count = lax.axis_size(axis)
    return lax.all_to_all(
        jnp.broadcast_to(shard[None], (count, *shard.shape)), axis, 0, 0, tiled=True
    )


def call(body, outs, args, specs=None, scratch=(), name=None):
    specs = specs or [ON_CHIP] * len(args)
    args = [
        arg if spec is SCALARS else pltpu.with_memory_space_constraint(arg, spec.memory_space)
        for arg, spec in zip(args, specs)
    ]
    return pl.pallas_call(
        body,
        out_shape=[pltpu.VMEM(shape, kind) for shape, kind in outs],
        in_specs=specs,
        out_specs=[ON_CHIP] * len(outs),
        scratch_shapes=list(scratch),
        compiler_params=pltpu.CompilerParams(vmem_limit_bytes=SCOPED_BYTES),
        name=name,
    )(*args)


def product(left, right):
    return jnp.dot(left, right, preferred_element_type=F32)


def first_solve(tree, sub_rhs, diag_inverse):
    rhs_count, depth = sub_rhs.shape[2:]
    cols = diag_inverse.shape[2]
    pieces = 3
    step = depth // pieces

    def body(tree_ref, rhs_hbm, inverse_hbm, out_ref, rhs, inverse, rhs_sem, inverse_sem):
        rhs_copy = pltpu.make_async_copy(rhs_hbm.at[tree_ref[0], 0], rhs, rhs_sem)
        rhs_copy.start()
        copies = []
        for piece in range(pieces):
            part = pl.ds(piece * step, step)
            copies.append(
                pltpu.make_async_copy(
                    inverse_hbm.at[0, part], inverse.at[part], inverse_sem.at[piece]
                )
            )
            copies[-1].start()
        rhs_copy.wait()
        total = jnp.zeros((rhs_count, cols), F32)
        for piece in range(pieces):
            copies[piece].wait()
            part = slice(piece * step, (piece + 1) * step)
            total = total + product(rhs[:, part].astype(BF16), inverse[part, :])
        out_ref[...] = total

    return call(
        body,
        [((rhs_count, cols), F32)],
        (tree, sub_rhs, diag_inverse),
        [SCALARS, IN_PLACE, IN_PLACE],
        [
            pltpu.VMEM((rhs_count, depth), F32),
            pltpu.VMEM((depth, cols), BF16),
            pltpu.SemaphoreType.DMA,
            pltpu.SemaphoreType.DMA((pieces,)),
        ],
        "first_solve",
    )[0]


def next_solve(place, rhs, sums, diag_inverse):
    def body(rhs_ref, *refs):
        *sum_refs, inverse_ref, out_ref = refs
        update = sum_refs[0][...]
        for ref in sum_refs[1:]:
            update = update + ref[...]
        residual = (rhs_ref[place] - update).astype(BF16)
        out_ref[...] = product(residual, inverse_ref[place])

    shape = (rhs.shape[1], diag_inverse.shape[2])
    return call(body, [(shape, F32)], (rhs, *sums, diag_inverse), name="next_solve")[0]


def mask_tiles(mask_ref, block, source, target):
    rows, cols = source.shape[1:]
    for i in range(rows // TILE):
        for j in range(cols // TILE):
            there = (
                block,
                slice(i * TILE, (i + 1) * TILE),
                slice(j * TILE, (j + 1) * TILE),
            )
            keep = jnp.full((TILE, TILE), mask_ref[block, i, j], F32).astype(BF16)
            target[there] = source[there] * keep


def stage(tree, mask, sub_rhs, diag_inverse, factor):
    levels, rhs_count, depth = sub_rhs.shape[1:]
    later = levels - 1
    cols = diag_inverse.shape[2]

    def body(
        tree_ref, mask_ref, rhs_hbm, inverse_hbm, factor_hbm, out_ref, inverse_ref, rhs_ref, landed, sems, other_sems
    ):
        blocks = factor_hbm.shape[0]
        copies = [
            pltpu.make_async_copy(factor_hbm.at[block], landed.at[block], sems.at[block])
            for block in range(blocks)
        ]
        others = [
            pltpu.make_async_copy(inverse_hbm.at[pl.ds(1, later)], inverse_ref, other_sems.at[0]),
            pltpu.make_async_copy(
                rhs_hbm.at[tree_ref[0], pl.ds(1, later)], rhs_ref, other_sems.at[1]
            ),
        ]
        for copy in copies + others:
            copy.start()
        for block, copy in enumerate(copies):
            copy.wait()
            mask_tiles(mask_ref, block, landed, out_ref)
        for copy in others:
            copy.wait()

    return call(
        body,
        [
            (factor.shape, BF16),
            ((later, depth, cols), BF16),
            ((later, rhs_count, depth), F32),
        ],
        (tree, mask, sub_rhs, diag_inverse, factor),
        [SCALARS, SCALARS, IN_PLACE, IN_PLACE, IN_PLACE],
        [
            pltpu.VMEM(factor.shape, BF16),
            pltpu.SemaphoreType.DMA((factor.shape[0],)),
            pltpu.SemaphoreType.DMA((2,)),
        ],
        "stage",
    )


def masked(mask, factor):
    def body(mask_ref, factor_ref, out_ref):
        for block in range(factor.shape[0]):
            mask_tiles(mask_ref, block, factor_ref, out_ref)

    return call(
        body, [(factor.shape, BF16)], (mask, factor), [SCALARS, ON_CHIP], name="masked"
    )[0]


def stacked(parts):
    def body(*refs):
        *part_refs, out_hbm, sems = refs
        copies = [
            pltpu.make_async_copy(ref, out_hbm.at[k], sems.at[k])
            for k, ref in enumerate(part_refs)
        ]
        for copy in copies:
            copy.start()
        for copy in copies:
            copy.wait()

    args = [pltpu.with_memory_space_constraint(part, pltpu.VMEM) for part in parts]
    return pl.pallas_call(
        body,
        out_shape=jax.ShapeDtypeStruct((len(parts), *parts[0].shape), F32),
        in_specs=[ON_CHIP] * len(parts),
        out_specs=IN_PLACE,
        scratch_shapes=[pltpu.SemaphoreType.DMA((len(parts),))],
        compiler_params=pltpu.CompilerParams(vmem_limit_bytes=SCOPED_BYTES),
        name="stacked",
    )(*args)


def kept_update(halves, factor, block, before):
    rows, cols = halves[0].shape
    out_cols = factor.shape[2]

    def body(one_ref, other_ref, factor_ref, *refs):
        *before_ref, solved_ref, kept_ref, out_ref = refs
        solved = one_ref[...] + other_ref[...]
        kept = solved.astype(BF16)
        solved_ref[...] = solved
        kept_ref[...] = kept
        update = product(kept, factor_ref[block])
        for ref in before_ref:
            update = update + ref[...]
        out_ref[...] = update

    return call(
        body,
        [((rows, cols), F32), ((rows, cols), BF16), ((rows, out_cols), F32)],
        (*halves, factor, *before),
        name="kept_update",
    )


def early_update(kept, factor, blocks):
    def body(*refs):
        *kept_refs, factor_ref, out_ref = refs
        update = product(kept_refs[0][...], factor_ref[blocks[0]])
        for ref, block in zip(kept_refs[1:], blocks[1:]):
            update = update + product(ref[...], factor_ref[block])
        out_ref[...] = update

    shape = (kept[0].shape[0], factor.shape[2])
    return call(body, [(shape, F32)], (*kept, factor), name="early_update")[0]


def root_part(rhs_rows, update_parts, root_inverse):
    def body(rhs_ref, one_ref, other_ref, inverse_ref, out_ref):
        residual = rhs_ref[...] - (one_ref[...] + other_ref[...])
        out_ref[...] = product(residual.astype(BF16), inverse_ref[...])

    shape = (rhs_rows.shape[0], root_inverse.shape[1])
    return call(
        body, [(shape, F32)], (rhs_rows, *update_parts, root_inverse), name="root_part"
    )[0]


def prow_halves(partial_sum):
    pair = partial_sum + partner(partial_sum, "core")
    return pair, partner(pair, "xl")


def owner_sums(partial_sum):
    pair = partial_sum + partner(partial_sum, "zl")
    return [pair] + [partner(pair, "y", bit) for bit in (2, 3, 1)]


def shards(
    sub_rhs, root_rhs, diag_inverse, root_inverse, inner_factor, inner_mask, root_factor, root_mask
):
    out_cols = inner_factor.shape[2]
    rhs_count = root_rhs.shape[0]
    tiles = out_cols // TILE
    tree = lax.axis_index("zt")
    first_tile = lax.axis_index(PROW) * tiles
    inner_tiles = lax.dynamic_slice_in_dim(inner_mask, first_tile, tiles, 2)
    root_tiles = lax.dynamic_slice_in_dim(root_mask, first_tile, tiles, 2)
    tree = tree.reshape(1)

    halves = prow_halves(first_solve(tree, sub_rhs, diag_inverse))
    inner, inverse, rhs = stage(tree, inner_tiles, sub_rhs, diag_inverse, inner_factor)
    root = masked(root_tiles, root_factor)
    solved0, kept0, update1 = kept_update(halves, inner, 0, ())
    halves = prow_halves(next_solve(0, rhs, owner_sums(update1), inverse))
    early = early_update((kept0,), inner, (1,))
    solved1, kept1, update2 = kept_update(halves, inner, 2, (early,))
    halves = prow_halves(next_solve(1, rhs, owner_sums(update2), inverse))
    early = early_update((kept0, kept1), root, (0, 1))
    solved2, _, root_local = kept_update(halves, root, 2, (early,))

    owners = lax.axis_size(OWN)
    few = rhs_count // owners
    own_rows = lax.all_to_all(
        root_local.reshape(owners, few, out_cols), OWN, 0, 0, tiled=True
    ).sum(axis=0)
    sub_solution, across = lax.optimization_barrier(
        (stacked([solved0, solved1, solved2]), partner(own_rows, "grid"))
    )
    total = own_rows + across
    total = total + partner(total, "zt", 1)
    rhs_rows = lax.dynamic_slice_in_dim(root_rhs, lax.axis_index(OWN) * few, few, 0)
    part = root_part(rhs_rows, (total, partner(total, "zt", 3)), root_inverse)
    pair, other = prow_halves(part)
    root_solution = to_everyone(pair + other, OWN).reshape(rhs_count, part.shape[1])
    return (sub_solution, root_solution)


def solution(mesh):
    prow, pcol = mesh.shape["prow"], mesh.shape["pcol"]
    cores, y = 2, 4
    trees = 8 // mesh.shape["grid"]
    fine = Mesh(
        mesh.devices.reshape(
            mesh.shape["grid"], prow // cores, cores, trees, pcol // (trees * y), y
        ),
        ("grid", "xl", "core", "zt", "zl", "y"),
    )
    columns = ("grid", "zt", "zl", "y")
    return jax.shard_map(
        shards,
        mesh=fine,
        in_specs=(
            P("grid", None, None, PROW),
            P(None, PROW),
            P(None, PROW, columns),
            P(PROW, "grid"),
            P(None, columns, PROW),
            P(None, columns, None),
            P(None, columns, PROW),
            P(None, columns, None),
        ),
        out_specs=(P(None, None, columns), P(None, "grid")),
        check_vma=False,
    )
```

```python
import jax
import jax.numpy as jnp
from jax import lax
from jax.experimental import pallas as pl
from jax.experimental.pallas import tpu as pltpu
from jax.sharding import Mesh
from jax.sharding import PartitionSpec as P

LEVELS = 3
TILE = 128
PROW = ("xl", "core")
OWN = ("zl", "y")
TREES = ("grid", "zt")
SCOPED_BYTES = 4 << 20
F32 = jnp.float32
BF16 = jnp.bfloat16

ON_CHIP = pl.BlockSpec(memory_space=pltpu.VMEM)
SCALARS = pl.BlockSpec(memory_space=pltpu.SMEM)
IN_PLACE = pl.BlockSpec(memory_space=pltpu.HBM)


def partner(shard, axis, bit=1):
    return lax.ppermute(shard, axis, [(i, i ^ bit) for i in range(lax.axis_size(axis))])


def to_everyone(shard, axis):
    count = lax.axis_size(axis)
    return lax.all_to_all(
        jnp.broadcast_to(shard[None], (count, *shard.shape)), axis, 0, 0, tiled=True
    )


def call(body, outs, args, specs=None, scratch=(), name=None):
    specs = specs or [ON_CHIP] * len(args)
    args = [
        arg if spec is SCALARS else pltpu.with_memory_space_constraint(arg, spec.memory_space)
        for arg, spec in zip(args, specs)
    ]
    return pl.pallas_call(
        body,
        out_shape=[pltpu.VMEM(shape, kind) for shape, kind in outs],
        in_specs=specs,
        out_specs=[ON_CHIP] * len(outs),
        scratch_shapes=list(scratch),
        compiler_params=pltpu.CompilerParams(vmem_limit_bytes=SCOPED_BYTES),
        name=name,
    )(*args)


def product(left, right):
    return jnp.dot(left, right, preferred_element_type=F32)


def first_solve(tree, sub_rhs, diag_inverse):
    rhs_count, depth = sub_rhs.shape[2:]
    cols = diag_inverse.shape[2]
    pieces = 3
    step = depth // pieces

    def body(tree_ref, rhs_hbm, inverse_hbm, out_ref, rhs, inverse, rhs_sem, inverse_sem):
        rhs_copy = pltpu.make_async_copy(rhs_hbm.at[tree_ref[0], 0], rhs, rhs_sem)
        rhs_copy.start()
        copies = []
        for piece in range(pieces):
            part = pl.ds(piece * step, step)
            copies.append(
                pltpu.make_async_copy(
                    inverse_hbm.at[0, part], inverse.at[part], inverse_sem.at[piece]
                )
            )
            copies[-1].start()
        rhs_copy.wait()
        total = jnp.zeros((rhs_count, cols), F32)
        for piece in range(pieces):
            copies[piece].wait()
            part = slice(piece * step, (piece + 1) * step)
            total = total + product(rhs[:, part].astype(BF16), inverse[part, :])
        out_ref[...] = total

    return call(
        body,
        [((rhs_count, cols), F32)],
        (tree, sub_rhs, diag_inverse),
        [SCALARS, IN_PLACE, IN_PLACE],
        [
            pltpu.VMEM((rhs_count, depth), F32),
            pltpu.VMEM((depth, cols), BF16),
            pltpu.SemaphoreType.DMA,
            pltpu.SemaphoreType.DMA((pieces,)),
        ],
        "first_solve",
    )[0]


def next_solve(place, rhs, sums, diag_inverse):
    def body(rhs_ref, *refs):
        *sum_refs, inverse_ref, out_ref = refs
        update = sum_refs[0][...]
        for ref in sum_refs[1:]:
            update = update + ref[...]
        residual = (rhs_ref[place] - update).astype(BF16)
        out_ref[...] = product(residual, inverse_ref[place])

    shape = (rhs.shape[1], diag_inverse.shape[2])
    return call(body, [(shape, F32)], (rhs, *sums, diag_inverse), name="next_solve")[0]


def mask_tiles(mask_ref, block, source, target):
    rows, cols = source.shape[1:]
    for i in range(rows // TILE):
        for j in range(cols // TILE):
            there = (
                block,
                slice(i * TILE, (i + 1) * TILE),
                slice(j * TILE, (j + 1) * TILE),
            )
            keep = jnp.full((TILE, TILE), mask_ref[block, i, j], F32).astype(BF16)
            target[there] = source[there] * keep


def stage(tree, mask, sub_rhs, diag_inverse, factor):
    levels, rhs_count, depth = sub_rhs.shape[1:]
    later = levels - 1
    cols = diag_inverse.shape[2]

    def body(
        tree_ref, mask_ref, rhs_hbm, inverse_hbm, factor_hbm, out_ref, inverse_ref, rhs_ref, landed, sems, other_sems
    ):
        blocks = factor_hbm.shape[0]
        copies = [
            pltpu.make_async_copy(factor_hbm.at[block], landed.at[block], sems.at[block])
            for block in range(blocks)
        ]
        others = [
            pltpu.make_async_copy(inverse_hbm.at[pl.ds(1, later)], inverse_ref, other_sems.at[0]),
            pltpu.make_async_copy(
                rhs_hbm.at[tree_ref[0], pl.ds(1, later)], rhs_ref, other_sems.at[1]
            ),
        ]
        for copy in copies + others:
            copy.start()
        for block, copy in enumerate(copies):
            copy.wait()
            mask_tiles(mask_ref, block, landed, out_ref)
        for copy in others:
            copy.wait()

    return call(
        body,
        [
            (factor.shape, BF16),
            ((later, depth, cols), BF16),
            ((later, rhs_count, depth), F32),
        ],
        (tree, mask, sub_rhs, diag_inverse, factor),
        [SCALARS, SCALARS, IN_PLACE, IN_PLACE, IN_PLACE],
        [
            pltpu.VMEM(factor.shape, BF16),
            pltpu.SemaphoreType.DMA((factor.shape[0],)),
            pltpu.SemaphoreType.DMA((2,)),
        ],
        "stage",
    )


def masked(mask, factor):
    def body(mask_ref, factor_ref, out_ref):
        for block in range(factor.shape[0]):
            mask_tiles(mask_ref, block, factor_ref, out_ref)

    return call(
        body, [(factor.shape, BF16)], (mask, factor), [SCALARS, ON_CHIP], name="masked"
    )[0]


def stacked(parts):
    def body(*refs):
        *part_refs, out_hbm, sems = refs
        copies = [
            pltpu.make_async_copy(ref, out_hbm.at[k], sems.at[k])
            for k, ref in enumerate(part_refs)
        ]
        for copy in copies:
            copy.start()
        for copy in copies:
            copy.wait()

    args = [pltpu.with_memory_space_constraint(part, pltpu.VMEM) for part in parts]
    return pl.pallas_call(
        body,
        out_shape=jax.ShapeDtypeStruct((len(parts), *parts[0].shape), F32),
        in_specs=[ON_CHIP] * len(parts),
        out_specs=IN_PLACE,
        scratch_shapes=[pltpu.SemaphoreType.DMA((len(parts),))],
        compiler_params=pltpu.CompilerParams(vmem_limit_bytes=SCOPED_BYTES),
        name="stacked",
    )(*args)


def kept_update(halves, factor, block, before, last=False):
    rows, cols = halves[0].shape
    out_cols = factor.shape[2]

    def body(one_ref, other_ref, factor_ref, *refs):
        before_ref, (out_ref, solved_ref, *kept_ref) = refs[: len(before)], refs[len(before) :]
        solved = one_ref[...] + other_ref[...]
        kept = solved.astype(BF16)
        solved_ref[...] = solved
        for ref in kept_ref:
            ref[...] = kept
        update = product(kept, factor_ref[block])
        for ref in before_ref:
            update = update + ref[...]
        out_ref[...] = update

    return call(
        body,
        [((rows, out_cols), F32), ((rows, cols), F32), ((rows, cols), BF16)][: 2 if last else 3],
        (*halves, factor, *before),
        name="kept_update",
    )


def early_update(kept, factor, blocks):
    def body(*refs):
        *kept_refs, factor_ref, out_ref = refs
        update = product(kept_refs[0][...], factor_ref[blocks[0]])
        for ref, block in zip(kept_refs[1:], blocks[1:]):
            update = update + product(ref[...], factor_ref[block])
        out_ref[...] = update

    shape = (kept[0].shape[0], factor.shape[2])
    return call(body, [(shape, F32)], (*kept, factor), name="early_update")[0]


def root_part(rhs_rows, update_parts, root_inverse):
    def body(rhs_ref, one_ref, other_ref, inverse_ref, out_ref):
        residual = rhs_ref[...] - (one_ref[...] + other_ref[...])
        out_ref[...] = product(residual.astype(BF16), inverse_ref[...])

    shape = (rhs_rows.shape[0], root_inverse.shape[1])
    return call(
        body, [(shape, F32)], (rhs_rows, *update_parts, root_inverse), name="root_part"
    )[0]


def prow_halves(partial_sum):
    pair = partial_sum + partner(partial_sum, "core")
    return pair, partner(pair, "xl")


def owner_sums(partial_sum):
    pair = partial_sum + partner(partial_sum, "zl")
    return [pair] + [partner(pair, "y", bit) for bit in (1, 3, 2)]


def shards(
    sub_rhs, root_rhs, diag_inverse, root_inverse, inner_factor, inner_mask, root_factor, root_mask
):
    out_cols = inner_factor.shape[2]
    rhs_count = root_rhs.shape[0]
    tiles = out_cols // TILE
    tree = lax.axis_index("zt")
    first_tile = lax.axis_index(PROW) * tiles
    inner_tiles = lax.dynamic_slice_in_dim(inner_mask, first_tile, tiles, 2)
    root_tiles = lax.dynamic_slice_in_dim(root_mask, first_tile, tiles, 2)
    tree = tree.reshape(1)

    halves = prow_halves(first_solve(tree, sub_rhs, diag_inverse))
    inner, inverse, rhs = stage(tree, inner_tiles, sub_rhs, diag_inverse, inner_factor)
    root = masked(root_tiles, root_factor)
    update1, solved0, kept0 = kept_update(halves, inner, 0, ())
    halves = prow_halves(next_solve(0, rhs, owner_sums(update1), inverse))
    early = early_update((kept0,), inner, (1,))
    update2, solved1, kept1 = kept_update(halves, inner, 2, (early,))
    halves = prow_halves(next_solve(1, rhs, owner_sums(update2), inverse))
    early = early_update((kept0, kept1), root, (0, 1))
    root_local, solved2 = kept_update(halves, root, 2, (early,), last=True)

    owners = lax.axis_size(OWN)
    few = rhs_count // owners
    own_rows = lax.all_to_all(
        root_local.reshape(owners, few, out_cols), OWN, 0, 0, tiled=True
    ).sum(axis=0)
    sub_solution, *arrived = lax.optimization_barrier(
        (
            stacked([solved0, solved1, solved2]),
            *[partner(own_rows, TREES, bit) for bit in (4, 1, 5)],
        )
    )
    total = own_rows + arrived[0] + (arrived[1] + arrived[2])
    rhs_rows = lax.dynamic_slice_in_dim(root_rhs, lax.axis_index(OWN) * few, few, 0)
    part = root_part(rhs_rows, (total, partner(total, "zt", 3)), root_inverse)
    pair, other = prow_halves(part)
    root_solution = to_everyone(pair + other, OWN).reshape(rhs_count, part.shape[1])
    return (sub_solution, root_solution)


def solution(mesh):
    prow, pcol = mesh.shape["prow"], mesh.shape["pcol"]
    cores, y = 2, 4
    trees = 8 // mesh.shape["grid"]
    fine = Mesh(
        mesh.devices.reshape(
            mesh.shape["grid"], prow // cores, cores, trees, pcol // (trees * y), y
        ),
        ("grid", "xl", "core", "zt", "zl", "y"),
    )
    columns = ("grid", "zt", "zl", "y")
    return jax.shard_map(
        shards,
        mesh=fine,
        in_specs=(
            P("grid", None, None, PROW),
            P(None, PROW),
            P(None, PROW, columns),
            P(PROW, "grid"),
            P(None, columns, PROW),
            P(None, columns, None),
            P(None, columns, PROW),
            P(None, columns, None),
        ),
        out_specs=(P(None, None, columns), P(None, "grid")),
        check_vma=False,
    )
```

```python
import jax
import jax.numpy as jnp
from jax import lax
from jax.experimental import pallas as pl
from jax.experimental.pallas import tpu as pltpu
from jax.sharding import Mesh
from jax.sharding import PartitionSpec as P

LEVELS = 3
TILE = 128
PARTS = 2
PROW = ("xl", "core")
OWN = ("zl", "y")
TREES = ("grid", "zt")
SCOPED_BYTES = 4 << 20
F32 = jnp.float32
BF16 = jnp.bfloat16

ON_CHIP = pl.BlockSpec(memory_space=pltpu.VMEM)
SCALARS = pl.BlockSpec(memory_space=pltpu.SMEM)
IN_PLACE = pl.BlockSpec(memory_space=pltpu.HBM)


def partner(shard, axis, bit=1):
    return lax.ppermute(shard, axis, [(i, i ^ bit) for i in range(lax.axis_size(axis))])


def to_everyone(shard, axis):
    count = lax.axis_size(axis)
    return lax.all_to_all(
        jnp.broadcast_to(shard[None], (count, *shard.shape)), axis, 0, 0, tiled=True
    )


def call(body, outs, args, specs=None, scratch=(), name=None):
    specs = specs or [ON_CHIP] * len(args)
    args = [
        arg if spec is SCALARS else pltpu.with_memory_space_constraint(arg, spec.memory_space)
        for arg, spec in zip(args, specs)
    ]
    return pl.pallas_call(
        body,
        out_shape=[pltpu.VMEM(shape, kind) for shape, kind in outs],
        in_specs=specs,
        out_specs=[ON_CHIP] * len(outs),
        scratch_shapes=list(scratch),
        compiler_params=pltpu.CompilerParams(vmem_limit_bytes=SCOPED_BYTES),
        name=name,
    )(*args)


def product(left, right):
    return jnp.dot(left, right, preferred_element_type=F32)


def first_solve(tree, sub_rhs, diag_inverse, parts):
    rhs_count, depth = sub_rhs.shape[2:]
    cols = diag_inverse.shape[2]
    pieces = 3
    step = depth // pieces

    few = rhs_count // parts

    def body(tree_ref, rhs_hbm, inverse_hbm, *refs):
        *out_refs, rhs, inverse, rhs_sem, inverse_sem = refs
        rhs_copy = pltpu.make_async_copy(rhs_hbm.at[tree_ref[0], 0], rhs, rhs_sem)
        rhs_copy.start()
        copies = []
        for piece in range(pieces):
            part = pl.ds(piece * step, step)
            copies.append(
                pltpu.make_async_copy(
                    inverse_hbm.at[0, part], inverse.at[part], inverse_sem.at[piece]
                )
            )
            copies[-1].start()
        rhs_copy.wait()
        total = jnp.zeros((rhs_count, cols), F32)
        for piece in range(pieces):
            copies[piece].wait()
            part = slice(piece * step, (piece + 1) * step)
            total = total + product(rhs[:, part].astype(BF16), inverse[part, :])
        for k, ref in enumerate(out_refs):
            ref[...] = total[k * few : (k + 1) * few]

    return call(
        body,
        [((few, cols), F32)] * parts,
        (tree, sub_rhs, diag_inverse),
        [SCALARS, IN_PLACE, IN_PLACE],
        [
            pltpu.VMEM((rhs_count, depth), F32),
            pltpu.VMEM((depth, cols), BF16),
            pltpu.SemaphoreType.DMA,
            pltpu.SemaphoreType.DMA((pieces,)),
        ],
        "first_solve",
    )


def next_solve(place, part, rhs, sums, diag_inverse):
    few = sums[0].shape[0]
    rows = slice(part * few, (part + 1) * few)

    def body(rhs_ref, *refs):
        *sum_refs, inverse_ref, out_ref = refs
        update = sum_refs[0][...]
        for ref in sum_refs[1:]:
            update = update + ref[...]
        residual = (rhs_ref[place, rows] - update).astype(BF16)
        out_ref[...] = product(residual, inverse_ref[place])

    shape = (few, diag_inverse.shape[2])
    return call(body, [(shape, F32)], (rhs, *sums, diag_inverse), name="next_solve")[0]


def mask_tiles(mask_ref, block, source, target):
    rows, cols = source.shape[1:]
    for i in range(rows // TILE):
        for j in range(cols // TILE):
            there = (
                block,
                slice(i * TILE, (i + 1) * TILE),
                slice(j * TILE, (j + 1) * TILE),
            )
            keep = jnp.full((TILE, TILE), mask_ref[block, i, j], F32).astype(BF16)
            target[there] = source[there] * keep


def stage(tree, mask, sub_rhs, diag_inverse, factor):
    levels, rhs_count, depth = sub_rhs.shape[1:]
    later = levels - 1
    cols = diag_inverse.shape[2]

    def body(
        tree_ref, mask_ref, rhs_hbm, inverse_hbm, factor_hbm, out_ref, inverse_ref, rhs_ref, landed, sems, other_sems
    ):
        blocks = factor_hbm.shape[0]
        copies = [
            pltpu.make_async_copy(factor_hbm.at[block], landed.at[block], sems.at[block])
            for block in range(blocks)
        ]
        others = [
            pltpu.make_async_copy(inverse_hbm.at[pl.ds(1, later)], inverse_ref, other_sems.at[0]),
            pltpu.make_async_copy(
                rhs_hbm.at[tree_ref[0], pl.ds(1, later)], rhs_ref, other_sems.at[1]
            ),
        ]
        for copy in copies + others:
            copy.start()
        for block, copy in enumerate(copies):
            copy.wait()
            mask_tiles(mask_ref, block, landed, out_ref)
        for copy in others:
            copy.wait()

    return call(
        body,
        [
            (factor.shape, BF16),
            ((later, depth, cols), BF16),
            ((later, rhs_count, depth), F32),
        ],
        (tree, mask, sub_rhs, diag_inverse, factor),
        [SCALARS, SCALARS, IN_PLACE, IN_PLACE, IN_PLACE],
        [
            pltpu.VMEM(factor.shape, BF16),
            pltpu.SemaphoreType.DMA((factor.shape[0],)),
            pltpu.SemaphoreType.DMA((2,)),
        ],
        "stage",
    )


def masked(mask, factor):
    def body(mask_ref, factor_ref, out_ref):
        for block in range(factor.shape[0]):
            mask_tiles(mask_ref, block, factor_ref, out_ref)

    return call(
        body, [(factor.shape, BF16)], (mask, factor), [SCALARS, ON_CHIP], name="masked"
    )[0]


def stacked(parts):
    levels, count = len(parts), len(parts[0])
    rows, cols = parts[0][0].shape

    def body(*refs):
        *part_refs, out_hbm, sems = refs
        copies = [
            pltpu.make_async_copy(
                ref, out_hbm.at[k // count, pl.ds(k % count * rows, rows)], sems.at[k]
            )
            for k, ref in enumerate(part_refs)
        ]
        for copy in copies:
            copy.start()
        for copy in copies:
            copy.wait()

    args = [pltpu.with_memory_space_constraint(part, pltpu.VMEM) for one in parts for part in one]
    return pl.pallas_call(
        body,
        out_shape=jax.ShapeDtypeStruct((levels, count * rows, cols), F32),
        in_specs=[ON_CHIP] * len(args),
        out_specs=IN_PLACE,
        scratch_shapes=[pltpu.SemaphoreType.DMA((len(args),))],
        compiler_params=pltpu.CompilerParams(vmem_limit_bytes=SCOPED_BYTES),
        name="stacked",
    )(*args)


def kept_update(halves, factor, block, before, last=False):
    rows, cols = halves[0].shape
    out_cols = factor.shape[2]

    def body(one_ref, other_ref, factor_ref, *refs):
        before_ref, (out_ref, solved_ref, *kept_ref) = refs[: len(before)], refs[len(before) :]
        solved = one_ref[...] + other_ref[...]
        kept = solved.astype(BF16)
        solved_ref[...] = solved
        for ref in kept_ref:
            ref[...] = kept
        update = product(kept, factor_ref[block])
        for ref in before_ref:
            update = update + ref[...]
        out_ref[...] = update

    return call(
        body,
        [((rows, out_cols), F32), ((rows, cols), F32), ((rows, cols), BF16)][: 2 if last else 3],
        (*halves, factor, *before),
        name="kept_update",
    )


def early_update(kept, factor, blocks):
    def body(*refs):
        *kept_refs, factor_ref, out_ref = refs
        update = product(kept_refs[0][...], factor_ref[blocks[0]])
        for ref, block in zip(kept_refs[1:], blocks[1:]):
            update = update + product(ref[...], factor_ref[block])
        out_ref[...] = update

    shape = (kept[0].shape[0], factor.shape[2])
    return call(body, [(shape, F32)], (*kept, factor), name="early_update")[0]


def root_part(rhs_rows, update_parts, root_inverse):
    def body(rhs_ref, one_ref, other_ref, inverse_ref, out_ref):
        residual = rhs_ref[...] - (one_ref[...] + other_ref[...])
        out_ref[...] = product(residual.astype(BF16), inverse_ref[...])

    shape = (rhs_rows.shape[0], root_inverse.shape[1])
    return call(
        body, [(shape, F32)], (rhs_rows, *update_parts, root_inverse), name="root_part"
    )[0]


def prow_halves(partial_sum):
    pair = partial_sum + partner(partial_sum, "core")
    return pair, partner(pair, "xl")


def owner_sums(partial_sum):
    pair = partial_sum + partner(partial_sum, "zl")
    return [pair] + [partner(pair, "y", bit) for bit in (1, 3, 2)]


def shards(
    sub_rhs, root_rhs, diag_inverse, root_inverse, inner_factor, inner_mask, root_factor, root_mask
):
    out_cols = inner_factor.shape[2]
    rhs_count = root_rhs.shape[0]
    tiles = out_cols // TILE
    tree = lax.axis_index("zt")
    first_tile = lax.axis_index(PROW) * tiles
    inner_tiles = lax.dynamic_slice_in_dim(inner_mask, first_tile, tiles, 2)
    root_tiles = lax.dynamic_slice_in_dim(root_mask, first_tile, tiles, 2)
    tree = tree.reshape(1)

    firsts = first_solve(tree, sub_rhs, diag_inverse, PARTS)
    inner, inverse, rhs = stage(tree, inner_tiles, sub_rhs, diag_inverse, inner_factor)
    root = masked(root_tiles, root_factor)
    solved, locals_ = [], []
    for part, first in enumerate(firsts):
        update, solved0, kept0 = kept_update(prow_halves(first), inner, 0, ())
        halves = prow_halves(next_solve(0, part, rhs, owner_sums(update), inverse))
        early = early_update((kept0,), inner, (1,))
        update, solved1, kept1 = kept_update(halves, inner, 2, (early,))
        halves = prow_halves(next_solve(1, part, rhs, owner_sums(update), inverse))
        early = early_update((kept0, kept1), root, (0, 1))
        root_local, solved2 = kept_update(halves, root, 2, (early,), last=True)
        solved.append((solved0, solved1, solved2))
        locals_.append(root_local)
    root_local = jnp.concatenate(locals_)

    owners = lax.axis_size(OWN)
    few = rhs_count // owners
    own_rows = lax.all_to_all(
        root_local.reshape(owners, few, out_cols), OWN, 0, 0, tiled=True
    ).sum(axis=0)
    sub_solution, *arrived = lax.optimization_barrier(
        (
            stacked(list(zip(*solved))),
            *[partner(own_rows, TREES, bit) for bit in (4, 1, 5)],
        )
    )
    total = own_rows + arrived[0] + (arrived[1] + arrived[2])
    rhs_rows = lax.dynamic_slice_in_dim(root_rhs, lax.axis_index(OWN) * few, few, 0)
    part = root_part(rhs_rows, (total, partner(total, "zt", 3)), root_inverse)
    pair, other = prow_halves(part)
    root_solution = to_everyone(pair + other, OWN).reshape(rhs_count, part.shape[1])
    return (sub_solution, root_solution)


def solution(mesh):
    prow, pcol = mesh.shape["prow"], mesh.shape["pcol"]
    cores, y = 2, 4
    trees = 8 // mesh.shape["grid"]
    fine = Mesh(
        mesh.devices.reshape(
            mesh.shape["grid"], prow // cores, cores, trees, pcol // (trees * y), y
        ),
        ("grid", "xl", "core", "zt", "zl", "y"),
    )
    columns = ("grid", "zt", "zl", "y")
    return jax.shard_map(
        shards,
        mesh=fine,
        in_specs=(
            P("grid", None, None, PROW),
            P(None, PROW),
            P(None, PROW, columns),
            P(PROW, "grid"),
            P(None, columns, PROW),
            P(None, columns, None),
            P(None, columns, PROW),
            P(None, columns, None),
        ),
        out_specs=(P(None, None, columns), P(None, "grid")),
        check_vma=False,
    )
```

```python
import jax
import jax.numpy as jnp
from jax import lax
from jax.experimental import pallas as pl
from jax.experimental.pallas import tpu as pltpu
from jax.sharding import Mesh
from jax.sharding import PartitionSpec as P

LEVELS = 3
TILE = 128
PARTS = 2
PROW = ("xl", "core")
OWN = ("zl", "y")
TREES = ("grid", "zt")
SCOPED_BYTES = 4 << 20
F32 = jnp.float32
BF16 = jnp.bfloat16

ON_CHIP = pl.BlockSpec(memory_space=pltpu.VMEM)
SCALARS = pl.BlockSpec(memory_space=pltpu.SMEM)
IN_PLACE = pl.BlockSpec(memory_space=pltpu.HBM)


def partner(shard, axis, bit=1):
    return lax.ppermute(shard, axis, [(i, i ^ bit) for i in range(lax.axis_size(axis))])


def to_everyone(shard, axis):
    count = lax.axis_size(axis)
    return lax.all_to_all(
        jnp.broadcast_to(shard[None], (count, *shard.shape)), axis, 0, 0, tiled=True
    )


def call(body, outs, args, specs=None, scratch=(), name=None):
    specs = specs or [ON_CHIP] * len(args)
    args = [
        arg if spec is SCALARS else pltpu.with_memory_space_constraint(arg, spec.memory_space)
        for arg, spec in zip(args, specs)
    ]
    return pl.pallas_call(
        body,
        out_shape=[pltpu.VMEM(shape, kind) for shape, kind in outs],
        in_specs=specs,
        out_specs=[ON_CHIP] * len(outs),
        scratch_shapes=list(scratch),
        compiler_params=pltpu.CompilerParams(vmem_limit_bytes=SCOPED_BYTES),
        name=name,
    )(*args)


def product(left, right):
    return jnp.dot(left, right, preferred_element_type=F32)


def first_solve(tree, sub_rhs, diag_inverse, parts):
    rhs_count, depth = sub_rhs.shape[2:]
    cols = diag_inverse.shape[2]
    pieces = 3
    step = depth // pieces

    few = rhs_count // parts

    def body(tree_ref, rhs_hbm, inverse_hbm, *refs):
        *out_refs, rhs, inverse, rhs_sem, inverse_sem = refs
        rhs_copy = pltpu.make_async_copy(rhs_hbm.at[tree_ref[0], 0], rhs, rhs_sem)
        rhs_copy.start()
        copies = []
        for piece in range(pieces):
            part = pl.ds(piece * step, step)
            copies.append(
                pltpu.make_async_copy(
                    inverse_hbm.at[0, part], inverse.at[part], inverse_sem.at[piece]
                )
            )
            copies[-1].start()
        rhs_copy.wait()
        total = jnp.zeros((rhs_count, cols), F32)
        for piece in range(pieces):
            copies[piece].wait()
            part = slice(piece * step, (piece + 1) * step)
            total = total + product(rhs[:, part].astype(BF16), inverse[part, :])
        for k, ref in enumerate(out_refs):
            ref[...] = total[k * few : (k + 1) * few]

    return call(
        body,
        [((few, cols), F32)] * parts,
        (tree, sub_rhs, diag_inverse),
        [SCALARS, IN_PLACE, IN_PLACE],
        [
            pltpu.VMEM((rhs_count, depth), F32),
            pltpu.VMEM((depth, cols), BF16),
            pltpu.SemaphoreType.DMA,
            pltpu.SemaphoreType.DMA((pieces,)),
        ],
        "first_solve",
    )


def next_solve(place, part, rhs, sums, diag_inverse):
    few = sums[0].shape[0]
    rows = slice(part * few, (part + 1) * few)

    def body(rhs_ref, *refs):
        *sum_refs, inverse_ref, out_ref = refs
        update = sum_refs[0][...]
        for ref in sum_refs[1:]:
            update = update + ref[...]
        residual = (rhs_ref[place, rows] - update).astype(BF16)
        out_ref[...] = product(residual, inverse_ref[place])

    shape = (few, diag_inverse.shape[2])
    return call(body, [(shape, F32)], (rhs, *sums, diag_inverse), name="next_solve")[0]


def mask_tiles(mask_ref, block, source, target):
    rows, cols = source.shape[1:]
    for i in range(rows // TILE):
        for j in range(cols // TILE):
            there = (
                block,
                slice(i * TILE, (i + 1) * TILE),
                slice(j * TILE, (j + 1) * TILE),
            )
            keep = jnp.full((TILE, TILE), mask_ref[block, i, j], F32).astype(BF16)
            target[there] = source[there] * keep


def stage(tree, mask, sub_rhs, diag_inverse, factor):
    levels, rhs_count, depth = sub_rhs.shape[1:]
    later = levels - 1
    cols = diag_inverse.shape[2]

    def body(
        tree_ref, mask_ref, rhs_hbm, inverse_hbm, factor_hbm, out_ref, inverse_ref, rhs_ref, landed, sems, other_sems
    ):
        blocks = factor_hbm.shape[0]
        copies = [
            pltpu.make_async_copy(factor_hbm.at[block], landed.at[block], sems.at[block])
            for block in range(blocks)
        ]
        others = [
            pltpu.make_async_copy(inverse_hbm.at[pl.ds(1, later)], inverse_ref, other_sems.at[0]),
            pltpu.make_async_copy(
                rhs_hbm.at[tree_ref[0], pl.ds(1, later)], rhs_ref, other_sems.at[1]
            ),
        ]
        for copy in copies + others:
            copy.start()
        for block, copy in enumerate(copies):
            copy.wait()
            mask_tiles(mask_ref, block, landed, out_ref)
        for copy in others:
            copy.wait()

    return call(
        body,
        [
            (factor.shape, BF16),
            ((later, depth, cols), BF16),
            ((later, rhs_count, depth), F32),
        ],
        (tree, mask, sub_rhs, diag_inverse, factor),
        [SCALARS, SCALARS, IN_PLACE, IN_PLACE, IN_PLACE],
        [
            pltpu.VMEM(factor.shape, BF16),
            pltpu.SemaphoreType.DMA((factor.shape[0],)),
            pltpu.SemaphoreType.DMA((2,)),
        ],
        "stage",
    )


def masked(mask, factor):
    def body(mask_ref, factor_ref, out_ref):
        for block in range(factor.shape[0]):
            mask_tiles(mask_ref, block, factor_ref, out_ref)

    return call(
        body, [(factor.shape, BF16)], (mask, factor), [SCALARS, ON_CHIP], name="masked"
    )[0]


def stacked(parts):
    levels, count = len(parts), len(parts[0])
    rows, cols = parts[0][0].shape

    def body(*refs):
        *part_refs, out_hbm, sems = refs
        copies = [
            pltpu.make_async_copy(
                ref, out_hbm.at[k // count, pl.ds(k % count * rows, rows)], sems.at[k]
            )
            for k, ref in enumerate(part_refs)
        ]
        for copy in copies:
            copy.start()
        for copy in copies:
            copy.wait()

    args = [pltpu.with_memory_space_constraint(part, pltpu.VMEM) for one in parts for part in one]
    return pl.pallas_call(
        body,
        out_shape=jax.ShapeDtypeStruct((levels, count * rows, cols), F32),
        in_specs=[ON_CHIP] * len(args),
        out_specs=IN_PLACE,
        scratch_shapes=[pltpu.SemaphoreType.DMA((len(args),))],
        compiler_params=pltpu.CompilerParams(vmem_limit_bytes=SCOPED_BYTES),
        name="stacked",
    )(*args)


def kept_update(halves, factor, block, before, last=False):
    rows, cols = halves[0].shape
    out_cols = factor.shape[2]

    def body(one_ref, other_ref, factor_ref, *refs):
        before_ref, (out_ref, solved_ref, *kept_ref) = refs[: len(before)], refs[len(before) :]
        solved = one_ref[...] + other_ref[...]
        kept = solved.astype(BF16)
        solved_ref[...] = solved
        for ref in kept_ref:
            ref[...] = kept
        update = product(kept, factor_ref[block])
        for ref in before_ref:
            update = update + ref[...]
        out_ref[...] = update

    return call(
        body,
        [((rows, out_cols), F32), ((rows, cols), F32), ((rows, cols), BF16)][: 2 if last else 3],
        (*halves, factor, *before),
        name="kept_update",
    )


def early_update(kept, factor, blocks):
    def body(*refs):
        *kept_refs, factor_ref, out_ref = refs
        update = product(kept_refs[0][...], factor_ref[blocks[0]])
        for ref, block in zip(kept_refs[1:], blocks[1:]):
            update = update + product(ref[...], factor_ref[block])
        out_ref[...] = update

    shape = (kept[0].shape[0], factor.shape[2])
    return call(body, [(shape, F32)], (*kept, factor), name="early_update")[0]


def root_part(rhs_rows, update_parts, root_inverse):
    def body(rhs_ref, own_ref, one_ref, two_ref, both_ref, inverse_ref, out_ref):
        update = own_ref[...] + one_ref[...] + (two_ref[...] + both_ref[...])
        residual = (rhs_ref[...] - update).astype(BF16)
        out_ref[...] = product(residual, inverse_ref[...])

    shape = (rhs_rows.shape[0], root_inverse.shape[1])
    return call(
        body, [(shape, F32)], (rhs_rows, *update_parts, root_inverse), name="root_part"
    )[0]


def prow_halves(partial_sum):
    pair = partial_sum + partner(partial_sum, "core")
    return pair, partner(pair, "xl")


def owner_sums(partial_sum):
    pair = partial_sum + partner(partial_sum, "zl")
    return [pair] + [partner(pair, "y", bit) for bit in (1, 3, 2)]


def shards(
    sub_rhs, root_rhs, diag_inverse, root_inverse, inner_factor, inner_mask, root_factor, root_mask
):
    out_cols = inner_factor.shape[2]
    rhs_count = root_rhs.shape[0]
    tiles = out_cols // TILE
    tree = lax.axis_index("zt")
    first_tile = lax.axis_index(PROW) * tiles
    inner_tiles = lax.dynamic_slice_in_dim(inner_mask, first_tile, tiles, 2)
    root_tiles = lax.dynamic_slice_in_dim(root_mask, first_tile, tiles, 2)
    tree = tree.reshape(1)

    firsts = first_solve(tree, sub_rhs, diag_inverse, PARTS)
    inner, inverse, rhs = stage(tree, inner_tiles, sub_rhs, diag_inverse, inner_factor)
    root = masked(root_tiles, root_factor)
    solved, locals_ = [], []
    for part, first in enumerate(firsts):
        update, solved0, kept0 = kept_update(prow_halves(first), inner, 0, ())
        halves = prow_halves(next_solve(0, part, rhs, owner_sums(update), inverse))
        early = early_update((kept0,), inner, (1,))
        update, solved1, kept1 = kept_update(halves, inner, 2, (early,))
        halves = prow_halves(next_solve(1, part, rhs, owner_sums(update), inverse))
        early = early_update((kept0, kept1), root, (0, 1))
        root_local, solved2 = kept_update(halves, root, 2, (early,), last=True)
        solved.append((solved0, solved1, solved2))
        locals_.append(root_local)
    root_local = jnp.concatenate(locals_)

    owners = lax.axis_size(OWN)
    few = rhs_count // owners
    rhs_rows = lax.dynamic_slice_in_dim(root_rhs, lax.axis_index(OWN) * few, few, 0)
    rhs_rows = jnp.where(lax.axis_index("zt") < lax.axis_size("zt") // 2, rhs_rows, 0.0)
    rhs_rows, root_local = lax.optimization_barrier((rhs_rows, root_local))
    own_rows = lax.all_to_all(
        root_local.reshape(owners, few, out_cols), OWN, 0, 0, tiled=True
    ).sum(axis=0)
    sub_solution, *arrived = lax.optimization_barrier(
        (
            stacked(list(zip(*solved))),
            *[partner(own_rows, TREES, bit) for bit in (4, 1, 5)],
        )
    )
    part = root_part(rhs_rows, (own_rows, *arrived), root_inverse)
    pair = part + partner(part, "core")
    trees = lax.axis_size("zt")
    across, far, both = [
        partner(pair, ("xl", "zt"), bit) for bit in (trees, trees - 1, 2 * trees - 1)
    ]
    own_solution = pair + across + (far + both)
    root_solution = to_everyone(own_solution, OWN).reshape(rhs_count, part.shape[1])
    return (sub_solution, root_solution)


def solution(mesh):
    prow, pcol = mesh.shape["prow"], mesh.shape["pcol"]
    cores, y = 2, 4
    trees = 8 // mesh.shape["grid"]
    fine = Mesh(
        mesh.devices.reshape(
            mesh.shape["grid"], prow // cores, cores, trees, pcol // (trees * y), y
        ),
        ("grid", "xl", "core", "zt", "zl", "y"),
    )
    columns = ("grid", "zt", "zl", "y")
    return jax.shard_map(
        shards,
        mesh=fine,
        in_specs=(
            P("grid", None, None, PROW),
            P(None, PROW),
            P(None, PROW, columns),
            P(PROW, "grid"),
            P(None, columns, PROW),
            P(None, columns, None),
            P(None, columns, PROW),
            P(None, columns, None),
        ),
        out_specs=(P(None, None, columns), P(None, "grid")),
        check_vma=False,
    )
```

```python
import jax
import jax.numpy as jnp
from jax import lax
from jax.experimental import pallas as pl
from jax.experimental.pallas import tpu as pltpu
from jax.sharding import Mesh
from jax.sharding import PartitionSpec as P

LEVELS = 3
TILE = 128
PARTS = 2
PROW = ("xl", "core")
OWN = ("zl", "y")
TREES = ("grid", "zt")
SCOPED_BYTES = 4 << 20
F32 = jnp.float32
BF16 = jnp.bfloat16

ON_CHIP = pl.BlockSpec(memory_space=pltpu.VMEM)
SCALARS = pl.BlockSpec(memory_space=pltpu.SMEM)
IN_PLACE = pl.BlockSpec(memory_space=pltpu.HBM)


def partner(shard, axis, bit=1):
    return lax.ppermute(shard, axis, [(i, i ^ bit) for i in range(lax.axis_size(axis))])


def to_everyone(shard, axis):
    count = lax.axis_size(axis)
    return lax.all_to_all(
        jnp.broadcast_to(shard[None], (count, *shard.shape)), axis, 0, 0, tiled=True
    )


def call(body, outs, args, specs=None, scratch=(), name=None):
    specs = specs or [ON_CHIP] * len(args)
    args = [
        arg if spec is SCALARS else pltpu.with_memory_space_constraint(arg, spec.memory_space)
        for arg, spec in zip(args, specs)
    ]
    return pl.pallas_call(
        body,
        out_shape=[pltpu.VMEM(shape, kind) for shape, kind in outs],
        in_specs=specs,
        out_specs=[ON_CHIP] * len(outs),
        scratch_shapes=list(scratch),
        compiler_params=pltpu.CompilerParams(vmem_limit_bytes=SCOPED_BYTES),
        name=name,
    )(*args)


def product(left, right):
    return jnp.dot(left, right, preferred_element_type=F32)


def first_solve(tree, sub_rhs, diag_inverse, parts):
    rhs_count, depth = sub_rhs.shape[2:]
    cols = diag_inverse.shape[2]
    pieces = 3
    step = depth // pieces

    few = rhs_count // parts

    def body(tree_ref, rhs_hbm, inverse_hbm, *refs):
        *out_refs, rhs, inverse, rhs_sem, inverse_sem = refs
        rhs_copy = pltpu.make_async_copy(rhs_hbm.at[tree_ref[0], 0], rhs, rhs_sem)
        rhs_copy.start()
        copies = []
        for piece in range(pieces):
            part = pl.ds(piece * step, step)
            copies.append(
                pltpu.make_async_copy(
                    inverse_hbm.at[0, part], inverse.at[part], inverse_sem.at[piece]
                )
            )
            copies[-1].start()
        rhs_copy.wait()
        total = jnp.zeros((rhs_count, cols), F32)
        for piece in range(pieces):
            copies[piece].wait()
            part = slice(piece * step, (piece + 1) * step)
            total = total + product(rhs[:, part].astype(BF16), inverse[part, :])
        for k, ref in enumerate(out_refs):
            ref[...] = total[k * few : (k + 1) * few]

    return call(
        body,
        [((few, cols), F32)] * parts,
        (tree, sub_rhs, diag_inverse),
        [SCALARS, IN_PLACE, IN_PLACE],
        [
            pltpu.VMEM((rhs_count, depth), F32),
            pltpu.VMEM((depth, cols), BF16),
            pltpu.SemaphoreType.DMA,
            pltpu.SemaphoreType.DMA((pieces,)),
        ],
        "first_solve",
    )


def next_solve(place, part, rhs, sums, diag_inverse):
    few = sums[0].shape[0]
    rows = slice(part * few, (part + 1) * few)

    def body(rhs_ref, *refs):
        *sum_refs, inverse_ref, out_ref = refs
        update = sum_refs[0][...]
        for ref in sum_refs[1:]:
            update = update + ref[...]
        residual = (rhs_ref[place, rows] - update).astype(BF16)
        out_ref[...] = product(residual, inverse_ref[place])

    shape = (few, diag_inverse.shape[2])
    return call(body, [(shape, F32)], (rhs, *sums, diag_inverse), name="next_solve")[0]


def mask_tiles(mask_ref, block, source, target):
    rows, cols = source.shape[1:]
    for i in range(rows // TILE):
        for j in range(cols // TILE):
            there = (
                block,
                slice(i * TILE, (i + 1) * TILE),
                slice(j * TILE, (j + 1) * TILE),
            )
            keep = jnp.full((TILE, TILE), mask_ref[block, i, j], F32).astype(BF16)
            target[there] = source[there] * keep


def stage(tree, mask, sub_rhs, diag_inverse, factor):
    levels, rhs_count, depth = sub_rhs.shape[1:]
    later = levels - 1
    cols = diag_inverse.shape[2]

    def body(
        tree_ref, mask_ref, rhs_hbm, inverse_hbm, factor_hbm, out_ref, inverse_ref, rhs_ref, landed, sems, other_sems
    ):
        blocks = factor_hbm.shape[0]
        copies = [
            pltpu.make_async_copy(factor_hbm.at[block], landed.at[block], sems.at[block])
            for block in range(blocks)
        ]
        others = [
            pltpu.make_async_copy(inverse_hbm.at[pl.ds(1, later)], inverse_ref, other_sems.at[0]),
            pltpu.make_async_copy(
                rhs_hbm.at[tree_ref[0], pl.ds(1, later)], rhs_ref, other_sems.at[1]
            ),
        ]
        for copy in copies + others:
            copy.start()
        for block, copy in enumerate(copies):
            copy.wait()
            mask_tiles(mask_ref, block, landed, out_ref)
        for copy in others:
            copy.wait()

    return call(
        body,
        [
            (factor.shape, BF16),
            ((later, depth, cols), BF16),
            ((later, rhs_count, depth), F32),
        ],
        (tree, mask, sub_rhs, diag_inverse, factor),
        [SCALARS, SCALARS, IN_PLACE, IN_PLACE, IN_PLACE],
        [
            pltpu.VMEM(factor.shape, BF16),
            pltpu.SemaphoreType.DMA((factor.shape[0],)),
            pltpu.SemaphoreType.DMA((2,)),
        ],
        "stage",
    )


def masked(mask, factor):
    def body(mask_ref, factor_ref, out_ref):
        for block in range(factor.shape[0]):
            mask_tiles(mask_ref, block, factor_ref, out_ref)

    return call(
        body, [(factor.shape, BF16)], (mask, factor), [SCALARS, ON_CHIP], name="masked"
    )[0]


def stacked(parts):
    levels, count = len(parts), len(parts[0])
    rows, cols = parts[0][0].shape

    def body(*refs):
        *part_refs, out_hbm, sems = refs
        copies = [
            pltpu.make_async_copy(
                ref, out_hbm.at[k // count, pl.ds(k % count * rows, rows)], sems.at[k]
            )
            for k, ref in enumerate(part_refs)
        ]
        for copy in copies:
            copy.start()
        for copy in copies:
            copy.wait()

    args = [pltpu.with_memory_space_constraint(part, pltpu.VMEM) for one in parts for part in one]
    return pl.pallas_call(
        body,
        out_shape=jax.ShapeDtypeStruct((levels, count * rows, cols), F32),
        in_specs=[ON_CHIP] * len(args),
        out_specs=IN_PLACE,
        scratch_shapes=[pltpu.SemaphoreType.DMA((len(args),))],
        compiler_params=pltpu.CompilerParams(vmem_limit_bytes=SCOPED_BYTES),
        name="stacked",
    )(*args)


def kept_update(halves, factor, block, before, last=False):
    rows, cols = halves[0].shape
    out_cols = factor.shape[2]

    def body(one_ref, other_ref, factor_ref, *refs):
        before_ref, (out_ref, solved_ref, *kept_ref) = refs[: len(before)], refs[len(before) :]
        solved = one_ref[...] + other_ref[...]
        kept = solved.astype(BF16)
        solved_ref[...] = solved
        for ref in kept_ref:
            ref[...] = kept
        update = product(kept, factor_ref[block])
        for ref in before_ref:
            update = update + ref[...]
        out_ref[...] = update

    return call(
        body,
        [((rows, out_cols), F32), ((rows, cols), F32), ((rows, cols), BF16)][: 2 if last else 3],
        (*halves, factor, *before),
        name="kept_update",
    )


def early_update(kept, factor, blocks):
    def body(*refs):
        *kept_refs, factor_ref, out_ref = refs
        update = product(kept_refs[0][...], factor_ref[blocks[0]])
        for ref, block in zip(kept_refs[1:], blocks[1:]):
            update = update + product(ref[...], factor_ref[block])
        out_ref[...] = update

    shape = (kept[0].shape[0], factor.shape[2])
    return call(body, [(shape, F32)], (*kept, factor), name="early_update")[0]


def root_part(rhs_rows, update, root_inverse):
    def body(rhs_ref, update_ref, inverse_ref, out_ref):
        residual = (rhs_ref[...] - update_ref[...]).astype(BF16)
        out_ref[...] = product(residual, inverse_ref[...])

    shape = (rhs_rows.shape[0], root_inverse.shape[1])
    return call(body, [(shape, F32)], (rhs_rows, update, root_inverse), name="root_part")[0]


def to_core1(shard):
    return lax.ppermute(shard, "core", [(0, 1)])


def to_core0(shard):
    return lax.ppermute(shard, "core", [(1, 0)])


def among_core1(shard, axis, bit=1):
    count, cores = lax.axis_size(axis), lax.axis_size("core")
    if axis in ("grid", "xl"):
        axes, where = (axis, "core"), lambda i: i * cores + 1
    else:
        axes, where = ("core", axis), lambda i: count + i
    return lax.ppermute(shard, axes, [(where(i), where(i ^ bit)) for i in range(count)])


def prow_halves(partial_sum):
    pair = partial_sum + partner(partial_sum, "core")
    return pair, partner(pair, "xl")


def owner_sums(partial_sum):
    pair = partial_sum + partner(partial_sum, "zl")
    return [pair] + [partner(pair, "y", bit) for bit in (1, 3, 2)]


def shards(
    sub_rhs, root_rhs, diag_inverse, root_inverse, inner_factor, inner_mask, root_factor, root_mask
):
    out_cols = inner_factor.shape[2]
    rhs_count = root_rhs.shape[0]
    tiles = out_cols // TILE
    tree = lax.axis_index("zt")
    first_tile = lax.axis_index(PROW) * tiles
    inner_tiles = lax.dynamic_slice_in_dim(inner_mask, first_tile, tiles, 2)
    root_tiles = lax.dynamic_slice_in_dim(root_mask, first_tile, tiles, 2)
    tree = tree.reshape(1)

    firsts = first_solve(tree, sub_rhs, diag_inverse, PARTS)
    inner, inverse, rhs = stage(tree, inner_tiles, sub_rhs, diag_inverse, inner_factor)
    root = masked(root_tiles, root_factor)
    solved, locals_ = [], []
    for part, first in enumerate(firsts):
        update, solved0, kept0 = kept_update(prow_halves(first), inner, 0, ())
        halves = prow_halves(next_solve(0, part, rhs, owner_sums(update), inverse))
        early = early_update((kept0,), inner, (1,))
        update, solved1, kept1 = kept_update(halves, inner, 2, (early,))
        halves = prow_halves(next_solve(1, part, rhs, owner_sums(update), inverse))
        early = early_update((kept0, kept1), root, (0, 1))
        root_local, solved2 = kept_update(halves, root, 2, (early,), last=True)
        solved.append((solved0, solved1, solved2))
        locals_.append(root_local)
    root_local = jnp.concatenate(locals_)

    owners = lax.axis_size(OWN)
    few = rhs_count // owners
    own_rows = lax.all_to_all(
        root_local.reshape(owners, few, out_cols), OWN, 0, 0, tiled=True
    ).sum(axis=0)
    both = jnp.concatenate([own_rows, to_core1(own_rows)])
    sub_solution, across = lax.optimization_barrier(
        (stacked(list(zip(*solved))), among_core1(both, "grid"))
    )
    total = both + across
    total = total + among_core1(total, "zt", 1)
    total = total + among_core1(total, "zt", 3)
    root_update = jnp.where(lax.axis_index("core") == 1, total[:few], to_core0(total[few:]))
    rhs_rows = lax.dynamic_slice_in_dim(root_rhs, lax.axis_index(OWN) * few, few, 0)
    pair, other = prow_halves(root_part(rhs_rows, root_update, root_inverse))
    root_solution = to_everyone(pair + other, OWN).reshape(rhs_count, pair.shape[1])
    return (sub_solution, root_solution)


def solution(mesh):
    prow, pcol = mesh.shape["prow"], mesh.shape["pcol"]
    cores, y = 2, 4
    trees = 8 // mesh.shape["grid"]
    fine = Mesh(
        mesh.devices.reshape(
            mesh.shape["grid"], prow // cores, cores, trees, pcol // (trees * y), y
        ),
        ("grid", "xl", "core", "zt", "zl", "y"),
    )
    columns = ("grid", "zt", "zl", "y")
    return jax.shard_map(
        shards,
        mesh=fine,
        in_specs=(
            P("grid", None, None, PROW),
            P(None, PROW),
            P(None, PROW, columns),
            P(PROW, "grid"),
            P(None, columns, PROW),
            P(None, columns, None),
            P(None, columns, PROW),
            P(None, columns, None),
        ),
        out_specs=(P(None, None, columns), P(None, "grid")),
        check_vma=False,
    )
```

```python
import jax
import jax.numpy as jnp
from jax import lax
from jax.experimental import pallas as pl
from jax.experimental.pallas import tpu as pltpu
from jax.sharding import Mesh
from jax.sharding import PartitionSpec as P

LEVELS = 3
TILE = 128
PARTS = 2
PROW = ("xl", "core")
OWN = "own"
TREES = ("grid", "zt")
SCOPED_BYTES = 4 << 20
F32 = jnp.float32
BF16 = jnp.bfloat16

ON_CHIP = pl.BlockSpec(memory_space=pltpu.VMEM)
SCALARS = pl.BlockSpec(memory_space=pltpu.SMEM)
IN_PLACE = pl.BlockSpec(memory_space=pltpu.HBM)


def partner(shard, axis, bit=1):
    return lax.ppermute(shard, axis, [(i, i ^ bit) for i in range(lax.axis_size(axis))])


def swap_blocks(blocks):
    order = list(range(lax.axis_size(OWN)))[::-1]
    return lax.all_to_all(blocks, OWN, 0, 0, axis_index_groups=[order], tiled=True)


def to_everyone(shard):
    count = lax.axis_size(OWN)
    return swap_blocks(jnp.broadcast_to(shard[None], (count, *shard.shape)))


def call(body, outs, args, specs=None, scratch=(), name=None):
    specs = specs or [ON_CHIP] * len(args)
    args = [
        arg if spec is SCALARS else pltpu.with_memory_space_constraint(arg, spec.memory_space)
        for arg, spec in zip(args, specs)
    ]
    return pl.pallas_call(
        body,
        out_shape=[pltpu.VMEM(shape, kind) for shape, kind in outs],
        in_specs=specs,
        out_specs=[ON_CHIP] * len(outs),
        scratch_shapes=list(scratch),
        compiler_params=pltpu.CompilerParams(vmem_limit_bytes=SCOPED_BYTES),
        name=name,
    )(*args)


def product(left, right):
    return jnp.dot(left, right, preferred_element_type=F32)


def first_solve(tree, sub_rhs, diag_inverse, parts):
    rhs_count, depth = sub_rhs.shape[2:]
    cols = diag_inverse.shape[2]
    pieces = 3
    step = depth // pieces

    few = rhs_count // parts

    def body(tree_ref, rhs_hbm, inverse_hbm, *refs):
        *out_refs, rhs, inverse, rhs_sem, inverse_sem = refs
        rhs_copy = pltpu.make_async_copy(rhs_hbm.at[tree_ref[0], 0], rhs, rhs_sem)
        rhs_copy.start()
        copies = []
        for piece in range(pieces):
            part = pl.ds(piece * step, step)
            copies.append(
                pltpu.make_async_copy(
                    inverse_hbm.at[0, part], inverse.at[part], inverse_sem.at[piece]
                )
            )
            copies[-1].start()
        rhs_copy.wait()
        total = jnp.zeros((rhs_count, cols), F32)
        for piece in range(pieces):
            copies[piece].wait()
            part = slice(piece * step, (piece + 1) * step)
            total = total + product(rhs[:, part].astype(BF16), inverse[part, :])
        for k, ref in enumerate(out_refs):
            ref[...] = total[k * few : (k + 1) * few]

    return call(
        body,
        [((few, cols), F32)] * parts,
        (tree, sub_rhs, diag_inverse),
        [SCALARS, IN_PLACE, IN_PLACE],
        [
            pltpu.VMEM((rhs_count, depth), F32),
            pltpu.VMEM((depth, cols), BF16),
            pltpu.SemaphoreType.DMA,
            pltpu.SemaphoreType.DMA((pieces,)),
        ],
        "first_solve",
    )


def next_solve(place, part, rhs, sums, diag_inverse):
    few = sums[0].shape[0]
    rows = slice(part * few, (part + 1) * few)

    def body(rhs_ref, *refs):
        *sum_refs, inverse_ref, out_ref = refs
        update = sum_refs[0][...]
        for ref in sum_refs[1:]:
            update = update + ref[...]
        residual = (rhs_ref[place, rows] - update).astype(BF16)
        out_ref[...] = product(residual, inverse_ref[place])

    shape = (few, diag_inverse.shape[2])
    return call(body, [(shape, F32)], (rhs, *sums, diag_inverse), name="next_solve")[0]


def mask_tiles(mask_ref, block, source, target):
    rows, cols = source.shape[1:]
    for i in range(rows // TILE):
        for j in range(cols // TILE):
            there = (
                block,
                slice(i * TILE, (i + 1) * TILE),
                slice(j * TILE, (j + 1) * TILE),
            )
            keep = jnp.full((TILE, TILE), mask_ref[block, i, j], F32).astype(BF16)
            target[there] = source[there] * keep


def stage(tree, mask, sub_rhs, diag_inverse, factor):
    levels, rhs_count, depth = sub_rhs.shape[1:]
    later = levels - 1
    cols = diag_inverse.shape[2]

    def body(
        tree_ref, mask_ref, rhs_hbm, inverse_hbm, factor_hbm, out_ref, inverse_ref, rhs_ref, landed, sems, other_sems
    ):
        blocks = factor_hbm.shape[0]
        copies = [
            pltpu.make_async_copy(factor_hbm.at[block], landed.at[block], sems.at[block])
            for block in range(blocks)
        ]
        others = [
            pltpu.make_async_copy(inverse_hbm.at[pl.ds(1, later)], inverse_ref, other_sems.at[0]),
            pltpu.make_async_copy(
                rhs_hbm.at[tree_ref[0], pl.ds(1, later)], rhs_ref, other_sems.at[1]
            ),
        ]
        for copy in copies + others:
            copy.start()
        for block, copy in enumerate(copies):
            copy.wait()
            mask_tiles(mask_ref, block, landed, out_ref)
        for copy in others:
            copy.wait()

    return call(
        body,
        [
            (factor.shape, BF16),
            ((later, depth, cols), BF16),
            ((later, rhs_count, depth), F32),
        ],
        (tree, mask, sub_rhs, diag_inverse, factor),
        [SCALARS, SCALARS, IN_PLACE, IN_PLACE, IN_PLACE],
        [
            pltpu.VMEM(factor.shape, BF16),
            pltpu.SemaphoreType.DMA((factor.shape[0],)),
            pltpu.SemaphoreType.DMA((2,)),
        ],
        "stage",
    )


def masked(mask, factor):
    def body(mask_ref, factor_ref, out_ref):
        for block in range(factor.shape[0]):
            mask_tiles(mask_ref, block, factor_ref, out_ref)

    return call(
        body, [(factor.shape, BF16)], (mask, factor), [SCALARS, ON_CHIP], name="masked"
    )[0]


def stacked(parts):
    levels, count = len(parts), len(parts[0])
    rows, cols = parts[0][0].shape

    def body(*refs):
        *part_refs, out_hbm, sems = refs
        copies = [
            pltpu.make_async_copy(
                ref, out_hbm.at[k // count, pl.ds(k % count * rows, rows)], sems.at[k]
            )
            for k, ref in enumerate(part_refs)
        ]
        for copy in copies:
            copy.start()
        for copy in copies:
            copy.wait()

    args = [pltpu.with_memory_space_constraint(part, pltpu.VMEM) for one in parts for part in one]
    return pl.pallas_call(
        body,
        out_shape=jax.ShapeDtypeStruct((levels, count * rows, cols), F32),
        in_specs=[ON_CHIP] * len(args),
        out_specs=IN_PLACE,
        scratch_shapes=[pltpu.SemaphoreType.DMA((len(args),))],
        compiler_params=pltpu.CompilerParams(vmem_limit_bytes=SCOPED_BYTES),
        name="stacked",
    )(*args)


def kept_update(halves, factor, block, before, last=False):
    rows, cols = halves[0].shape
    out_cols = factor.shape[2]

    def body(one_ref, other_ref, factor_ref, *refs):
        before_ref, (out_ref, solved_ref, *kept_ref) = refs[: len(before)], refs[len(before) :]
        solved = one_ref[...] + other_ref[...]
        kept = solved.astype(BF16)
        solved_ref[...] = solved
        for ref in kept_ref:
            ref[...] = kept
        update = product(kept, factor_ref[block])
        for ref in before_ref:
            update = update + ref[...]
        out_ref[...] = update

    return call(
        body,
        [((rows, out_cols), F32), ((rows, cols), F32), ((rows, cols), BF16)][: 2 if last else 3],
        (*halves, factor, *before),
        name="kept_update",
    )


def early_update(kept, factor, blocks):
    def body(*refs):
        *kept_refs, factor_ref, out_ref = refs
        update = product(kept_refs[0][...], factor_ref[blocks[0]])
        for ref, block in zip(kept_refs[1:], blocks[1:]):
            update = update + product(ref[...], factor_ref[block])
        out_ref[...] = update

    shape = (kept[0].shape[0], factor.shape[2])
    return call(body, [(shape, F32)], (*kept, factor), name="early_update")[0]


def root_part(rhs_rows, update_parts, root_inverse):
    def body(rhs_ref, one_ref, other_ref, inverse_ref, out_ref):
        residual = rhs_ref[...] - (one_ref[...] + other_ref[...])
        out_ref[...] = product(residual.astype(BF16), inverse_ref[...])

    shape = (rhs_rows.shape[0], root_inverse.shape[1])
    return call(
        body, [(shape, F32)], (rhs_rows, *update_parts, root_inverse), name="root_part"
    )[0]


def prow_halves(partial_sum):
    pair = partial_sum + partner(partial_sum, "core")
    return pair, partner(pair, "xl")


def owner_sums(partial_sum):
    pair = partial_sum + partner(partial_sum, OWN, 4)
    return [pair] + [partner(pair, OWN, bit) for bit in (2, 3, 1)]


def shards(
    sub_rhs, root_rhs, diag_inverse, root_inverse, inner_factor, inner_mask, root_factor, root_mask
):
    out_cols = inner_factor.shape[2]
    rhs_count = root_rhs.shape[0]
    tiles = out_cols // TILE
    tree = lax.axis_index("zt")
    first_tile = lax.axis_index(PROW) * tiles
    inner_tiles = lax.dynamic_slice_in_dim(inner_mask, first_tile, tiles, 2)
    root_tiles = lax.dynamic_slice_in_dim(root_mask, first_tile, tiles, 2)
    tree = tree.reshape(1)

    firsts = first_solve(tree, sub_rhs, diag_inverse, PARTS)
    inner, inverse, rhs = stage(tree, inner_tiles, sub_rhs, diag_inverse, inner_factor)
    root = masked(root_tiles, root_factor)
    solved, locals_ = [], []
    for part, first in enumerate(firsts):
        update, solved0, kept0 = kept_update(prow_halves(first), inner, 0, ())
        halves = prow_halves(next_solve(0, part, rhs, owner_sums(update), inverse))
        early = early_update((kept0,), inner, (1,))
        update, solved1, kept1 = kept_update(halves, inner, 2, (early,))
        halves = prow_halves(next_solve(1, part, rhs, owner_sums(update), inverse))
        early = early_update((kept0, kept1), root, (0, 1))
        root_local, solved2 = kept_update(halves, root, 2, (early,), last=True)
        solved.append((solved0, solved1, solved2))
        locals_.append(root_local)
    root_local = jnp.concatenate(locals_)

    owners = lax.axis_size(OWN)
    few = rhs_count // owners
    place = owners - 1 - lax.axis_index(OWN)
    own_rows = swap_blocks(root_local.reshape(owners, few, out_cols)).sum(axis=0)
    sub_solution, *arrived = lax.optimization_barrier(
        (
            stacked(list(zip(*solved))),
            *[partner(own_rows, TREES, bit) for bit in (4, 1, 5)],
        )
    )
    total = own_rows + arrived[0] + (arrived[1] + arrived[2])
    rhs_rows = lax.dynamic_slice_in_dim(root_rhs, place * few, few, 0)
    part = root_part(rhs_rows, (total, partner(total, "zt", 3)), root_inverse)
    pair, other = prow_halves(part)
    root_solution = to_everyone(pair + other).reshape(rhs_count, part.shape[1])
    return (sub_solution, root_solution)


def solution(mesh):
    prow, pcol = mesh.shape["prow"], mesh.shape["pcol"]
    cores = 2
    trees = 8 // mesh.shape["grid"]
    fine = Mesh(
        mesh.devices.reshape(
            mesh.shape["grid"], prow // cores, cores, trees, pcol // trees
        ),
        ("grid", "xl", "core", "zt", "own"),
    )
    columns = ("grid", "zt", "own")
    return jax.shard_map(
        shards,
        mesh=fine,
        in_specs=(
            P("grid", None, None, PROW),
            P(None, PROW),
            P(None, PROW, columns),
            P(PROW, "grid"),
            P(None, columns, PROW),
            P(None, columns, None),
            P(None, columns, PROW),
            P(None, columns, None),
        ),
        out_specs=(P(None, None, columns), P(None, "grid")),
        check_vma=False,
    )
```

```python
import jax
import jax.numpy as jnp
from jax import lax
from jax.experimental import pallas as pl
from jax.experimental.pallas import tpu as pltpu
from jax.sharding import Mesh
from jax.sharding import PartitionSpec as P

LEVELS = 3
TILE = 128
PARTS = 2
PROW = ("xl", "core")
OWN = "own"
SCOPED_BYTES = 4 << 20
F32 = jnp.float32
BF16 = jnp.bfloat16

ON_CHIP = pl.BlockSpec(memory_space=pltpu.VMEM)
SCALARS = pl.BlockSpec(memory_space=pltpu.SMEM)
IN_PLACE = pl.BlockSpec(memory_space=pltpu.HBM)


def partner(shard, axis, bit=1):
    return lax.ppermute(shard, axis, [(i, i ^ bit) for i in range(lax.axis_size(axis))])


def swap_blocks(blocks):
    order = list(range(lax.axis_size(OWN)))[::-1]
    return lax.all_to_all(blocks, OWN, 0, 0, axis_index_groups=[order], tiled=True)


def to_everyone(shard):
    count = lax.axis_size(OWN)
    return swap_blocks(jnp.broadcast_to(shard[None], (count, *shard.shape)))


def call(body, outs, args, specs=None, scratch=(), name=None):
    specs = specs or [ON_CHIP] * len(args)
    args = [
        arg if spec is SCALARS else pltpu.with_memory_space_constraint(arg, spec.memory_space)
        for arg, spec in zip(args, specs)
    ]
    return pl.pallas_call(
        body,
        out_shape=[pltpu.VMEM(shape, kind) for shape, kind in outs],
        in_specs=specs,
        out_specs=[ON_CHIP] * len(outs),
        scratch_shapes=list(scratch),
        compiler_params=pltpu.CompilerParams(vmem_limit_bytes=SCOPED_BYTES),
        name=name,
    )(*args)


def product(left, right):
    return jnp.dot(left, right, preferred_element_type=F32)


def first_solve(tree, sub_rhs, diag_inverse):
    rhs_count, depth = sub_rhs.shape[2:]
    cols = diag_inverse.shape[2]
    pieces = 3
    step = depth // pieces

    def body(tree_ref, rhs_hbm, inverse_hbm, out_ref, rhs, inverse, rhs_sem, inverse_sem):
        rhs_copy = pltpu.make_async_copy(rhs_hbm.at[tree_ref[0], 0], rhs, rhs_sem)
        rhs_copy.start()
        copies = []
        for piece in range(pieces):
            part = pl.ds(piece * step, step)
            copies.append(
                pltpu.make_async_copy(
                    inverse_hbm.at[0, part], inverse.at[part], inverse_sem.at[piece]
                )
            )
            copies[-1].start()
        rhs_copy.wait()
        total = jnp.zeros((rhs_count, cols), F32)
        for piece in range(pieces):
            copies[piece].wait()
            part = slice(piece * step, (piece + 1) * step)
            total = total + product(rhs[:, part].astype(BF16), inverse[part, :])
        out_ref[...] = total

    return call(
        body,
        [((rhs_count, cols), F32)],
        (tree, sub_rhs, diag_inverse),
        [SCALARS, IN_PLACE, IN_PLACE],
        [
            pltpu.VMEM((rhs_count, depth), F32),
            pltpu.VMEM((depth, cols), BF16),
            pltpu.SemaphoreType.DMA,
            pltpu.SemaphoreType.DMA((pieces,)),
        ],
        "first_solve",
    )[0]


def next_solve(place, part, rhs, sums, diag_inverse):
    few = sums[0].shape[0]
    rows = slice(part * few, (part + 1) * few)

    def body(rhs_ref, *refs):
        *sum_refs, inverse_ref, out_ref = refs
        update = sum_refs[0][...]
        for ref in sum_refs[1:]:
            update = update + ref[...]
        residual = (rhs_ref[place, rows] - update).astype(BF16)
        out_ref[...] = product(residual, inverse_ref[place])

    shape = (few, diag_inverse.shape[2])
    return call(body, [(shape, F32)], (rhs, *sums, diag_inverse), name="next_solve")[0]


def mask_tiles(mask_ref, block, source, target):
    rows, cols = source.shape[1:]
    for i in range(rows // TILE):
        for j in range(cols // TILE):
            there = (
                block,
                slice(i * TILE, (i + 1) * TILE),
                slice(j * TILE, (j + 1) * TILE),
            )
            keep = jnp.full((TILE, TILE), mask_ref[block, i, j], F32).astype(BF16)
            target[there] = source[there] * keep


def stage(tree, mask, sub_rhs, diag_inverse, factor):
    levels, rhs_count, depth = sub_rhs.shape[1:]
    later = levels - 1
    cols = diag_inverse.shape[2]

    def body(
        tree_ref, mask_ref, rhs_hbm, inverse_hbm, factor_hbm, out_ref, inverse_ref, rhs_ref, landed, sems, other_sems
    ):
        blocks = factor_hbm.shape[0]
        copies = [
            pltpu.make_async_copy(factor_hbm.at[block], landed.at[block], sems.at[block])
            for block in range(blocks)
        ]
        others = [
            pltpu.make_async_copy(inverse_hbm.at[pl.ds(1, later)], inverse_ref, other_sems.at[0]),
            pltpu.make_async_copy(
                rhs_hbm.at[tree_ref[0], pl.ds(1, later)], rhs_ref, other_sems.at[1]
            ),
        ]
        for copy in copies + others:
            copy.start()
        for block, copy in enumerate(copies):
            copy.wait()
            mask_tiles(mask_ref, block, landed, out_ref)
        for copy in others:
            copy.wait()

    return call(
        body,
        [
            (factor.shape, BF16),
            ((later, depth, cols), BF16),
            ((later, rhs_count, depth), F32),
        ],
        (tree, mask, sub_rhs, diag_inverse, factor),
        [SCALARS, SCALARS, IN_PLACE, IN_PLACE, IN_PLACE],
        [
            pltpu.VMEM(factor.shape, BF16),
            pltpu.SemaphoreType.DMA((factor.shape[0],)),
            pltpu.SemaphoreType.DMA((2,)),
        ],
        "stage",
    )


def masked(mask, factor):
    def body(mask_ref, factor_ref, out_ref):
        for block in range(factor.shape[0]):
            mask_tiles(mask_ref, block, factor_ref, out_ref)

    return call(
        body, [(factor.shape, BF16)], (mask, factor), [SCALARS, ON_CHIP], name="masked"
    )[0]


def stacked(parts):
    levels, count = len(parts), len(parts[0])
    rows, cols = parts[0][0].shape

    def body(*refs):
        *part_refs, out_hbm, sems = refs
        copies = [
            pltpu.make_async_copy(
                ref, out_hbm.at[k // count, pl.ds(k % count * rows, rows)], sems.at[k]
            )
            for k, ref in enumerate(part_refs)
        ]
        for copy in copies:
            copy.start()
        for copy in copies:
            copy.wait()

    args = [pltpu.with_memory_space_constraint(part, pltpu.VMEM) for one in parts for part in one]
    return pl.pallas_call(
        body,
        out_shape=jax.ShapeDtypeStruct((levels, count * rows, cols), F32),
        in_specs=[ON_CHIP] * len(args),
        out_specs=IN_PLACE,
        scratch_shapes=[pltpu.SemaphoreType.DMA((len(args),))],
        compiler_params=pltpu.CompilerParams(vmem_limit_bytes=SCOPED_BYTES),
        name="stacked",
    )(*args)


def kept_update(halves, factor, block, before, parts=1, last=False):
    rows, cols = halves[0].shape
    out_cols = factor.shape[2]
    few = rows // parts
    places = [slice(k * few, (k + 1) * few) for k in range(parts)]

    def body(one_ref, other_ref, factor_ref, *refs):
        before_refs, outs = refs[: len(before)], refs[len(before) :]
        solved = one_ref[...] + other_ref[...]
        kept = solved.astype(BF16)
        update = product(kept, factor_ref[block])
        for ref in before_refs:
            update = update + ref[...]
        for k, whole in enumerate((update, solved, kept)):
            for ref, place in zip(outs[k * parts : (k + 1) * parts], places):
                ref[...] = whole[place]

    kinds = [((few, out_cols), F32), ((few, cols), F32), ((few, cols), BF16)]
    outs = [kind for kind in kinds[: 2 if last else 3] for _ in range(parts)]
    return call(body, outs, (*halves, factor, *before), name="kept_update")


def early_update(kept, factor, blocks):
    def body(*refs):
        *kept_refs, factor_ref, out_ref = refs
        update = product(kept_refs[0][...], factor_ref[blocks[0]])
        for ref, block in zip(kept_refs[1:], blocks[1:]):
            update = update + product(ref[...], factor_ref[block])
        out_ref[...] = update

    shape = (kept[0].shape[0], factor.shape[2])
    return call(body, [(shape, F32)], (*kept, factor), name="early_update")[0]


def root_part(rhs_rows, update_parts, root_inverse):
    def body(rhs_ref, one_ref, other_ref, inverse_ref, out_ref):
        residual = rhs_ref[...] - (one_ref[...] + other_ref[...])
        out_ref[...] = product(residual.astype(BF16), inverse_ref[...])

    shape = (rhs_rows.shape[0], root_inverse.shape[1])
    return call(
        body, [(shape, F32)], (rhs_rows, *update_parts, root_inverse), name="root_part"
    )[0]


def prow_halves(partial_sum):
    pair = partial_sum + partner(partial_sum, "core")
    return pair, partner(pair, "xl")


def owner_sums(partial_sum):
    pair = partial_sum + partner(partial_sum, OWN, 4)
    return [pair] + [partner(pair, OWN, bit) for bit in (2, 3, 1)]


def shards(
    sub_rhs, root_rhs, diag_inverse, root_inverse, inner_factor, inner_mask, root_factor, root_mask
):
    out_cols = inner_factor.shape[2]
    rhs_count = root_rhs.shape[0]
    tiles = out_cols // TILE
    tree = lax.axis_index("zt")
    first_tile = lax.axis_index(PROW) * tiles
    inner_tiles = lax.dynamic_slice_in_dim(inner_mask, first_tile, tiles, 2)
    root_tiles = lax.dynamic_slice_in_dim(root_mask, first_tile, tiles, 2)
    tree = tree.reshape(1)

    halves = prow_halves(first_solve(tree, sub_rhs, diag_inverse))
    inner, inverse, rhs = stage(tree, inner_tiles, sub_rhs, diag_inverse, inner_factor)
    root = masked(root_tiles, root_factor)
    solved, locals_ = [], []
    outs = kept_update(halves, inner, 0, (), PARTS)
    for part in range(PARTS):
        update, solved0, kept0 = outs[part::PARTS]
        halves = prow_halves(next_solve(0, part, rhs, owner_sums(update), inverse))
        early = early_update((kept0,), inner, (1,))
        update, solved1, kept1 = kept_update(halves, inner, 2, (early,))
        halves = prow_halves(next_solve(1, part, rhs, owner_sums(update), inverse))
        early = early_update((kept0, kept1), root, (0, 1))
        root_local, solved2 = kept_update(halves, root, 2, (early,), last=True)
        solved.append((solved0, solved1, solved2))
        locals_.append(root_local)
    root_local = jnp.concatenate(locals_)

    owners = lax.axis_size(OWN)
    few = rhs_count // owners
    place = owners - 1 - lax.axis_index(OWN)
    own_rows = swap_blocks(root_local.reshape(owners, few, out_cols)).sum(axis=0)
    sub_solution, across = lax.optimization_barrier(
        (stacked(list(zip(*solved))), partner(own_rows, "grid"))
    )
    total = own_rows + across
    total = total + partner(total, "zt", 1)
    rhs_rows = lax.dynamic_slice_in_dim(root_rhs, place * few, few, 0)
    part = root_part(rhs_rows, (total, partner(total, "zt", 3)), root_inverse)
    pair, other = prow_halves(part)
    root_solution = to_everyone(pair + other).reshape(rhs_count, part.shape[1])
    return (sub_solution, root_solution)


def solution(mesh):
    prow, pcol = mesh.shape["prow"], mesh.shape["pcol"]
    cores = 2
    trees = 8 // mesh.shape["grid"]
    fine = Mesh(
        mesh.devices.reshape(
            mesh.shape["grid"], prow // cores, cores, trees, pcol // trees
        ),
        ("grid", "xl", "core", "zt", "own"),
    )
    columns = ("grid", "zt", "own")
    return jax.shard_map(
        shards,
        mesh=fine,
        in_specs=(
            P("grid", None, None, PROW),
            P(None, PROW),
            P(None, PROW, columns),
            P(PROW, "grid"),
            P(None, columns, PROW),
            P(None, columns, None),
            P(None, columns, PROW),
            P(None, columns, None),
        ),
        out_specs=(P(None, None, columns), P(None, "grid")),
        check_vma=False,
    )
```

```python
import jax
import jax.numpy as jnp
from jax import lax
from jax.experimental import pallas as pl
from jax.experimental.pallas import tpu as pltpu
from jax.sharding import Mesh
from jax.sharding import PartitionSpec as P

LEVELS = 3
TILE = 128
PARTS = 2
PROW = ("xl", "core")
PCOL = "pcol"
SUBTREES = 8
SCOPED_BYTES = 4 << 20
F32 = jnp.float32
BF16 = jnp.bfloat16

ON_CHIP = pl.BlockSpec(memory_space=pltpu.VMEM)
SCALARS = pl.BlockSpec(memory_space=pltpu.SMEM)
IN_PLACE = pl.BlockSpec(memory_space=pltpu.HBM)


def partner(shard, axis, bit=1):
    return lax.ppermute(shard, axis, [(i, i ^ bit) for i in range(lax.axis_size(axis))])


def to_everyone(shard, axis):
    count = lax.axis_size(axis)
    return lax.all_to_all(
        jnp.broadcast_to(shard[None], (count, *shard.shape)), axis, 0, 0, tiled=True
    )


def call(body, outs, args, specs=None, scratch=(), name=None):
    specs = specs or [ON_CHIP] * len(args)
    args = [
        arg if spec is SCALARS else pltpu.with_memory_space_constraint(arg, spec.memory_space)
        for arg, spec in zip(args, specs)
    ]
    return pl.pallas_call(
        body,
        out_shape=[pltpu.VMEM(shape, kind) for shape, kind in outs],
        in_specs=specs,
        out_specs=[ON_CHIP] * len(outs),
        scratch_shapes=list(scratch),
        compiler_params=pltpu.CompilerParams(vmem_limit_bytes=SCOPED_BYTES),
        name=name,
    )(*args)


def product(left, right):
    return jnp.dot(left, right, preferred_element_type=F32)


def first_solve(tree, sub_rhs, diag_inverse):
    rhs_count, depth = sub_rhs.shape[2:]
    cols = diag_inverse.shape[2]
    pieces = 3
    step = depth // pieces

    def body(tree_ref, rhs_hbm, inverse_hbm, out_ref, rhs, inverse, rhs_sem, inverse_sem):
        rhs_copy = pltpu.make_async_copy(rhs_hbm.at[tree_ref[0], 0], rhs, rhs_sem)
        rhs_copy.start()
        copies = []
        for piece in range(pieces):
            part = pl.ds(piece * step, step)
            copies.append(
                pltpu.make_async_copy(
                    inverse_hbm.at[0, part], inverse.at[part], inverse_sem.at[piece]
                )
            )
            copies[-1].start()
        rhs_copy.wait()
        total = jnp.zeros((rhs_count, cols), F32)
        for piece in range(pieces):
            copies[piece].wait()
            part = slice(piece * step, (piece + 1) * step)
            total = total + product(rhs[:, part].astype(BF16), inverse[part, :])
        out_ref[...] = total

    return call(
        body,
        [((rhs_count, cols), F32)],
        (tree, sub_rhs, diag_inverse),
        [SCALARS, IN_PLACE, IN_PLACE],
        [
            pltpu.VMEM((rhs_count, depth), F32),
            pltpu.VMEM((depth, cols), BF16),
            pltpu.SemaphoreType.DMA,
            pltpu.SemaphoreType.DMA((pieces,)),
        ],
        "first_solve",
    )[0]


def next_solve(place, part, rhs, sums, diag_inverse):
    few = sums[0].shape[0]
    rows = slice(part * few, (part + 1) * few)

    def body(rhs_ref, *refs):
        *sum_refs, inverse_ref, out_ref = refs
        update = sum_refs[0][...]
        for ref in sum_refs[1:]:
            update = update + ref[...]
        residual = (rhs_ref[place, rows] - update).astype(BF16)
        out_ref[...] = product(residual, inverse_ref[place])

    shape = (few, diag_inverse.shape[2])
    return call(body, [(shape, F32)], (rhs, *sums, diag_inverse), name="next_solve")[0]


def mask_tiles(mask_ref, block, source, target):
    rows, cols = source.shape[1:]
    for i in range(rows // TILE):
        for j in range(cols // TILE):
            there = (
                block,
                slice(i * TILE, (i + 1) * TILE),
                slice(j * TILE, (j + 1) * TILE),
            )
            keep = jnp.full((TILE, TILE), mask_ref[block, i, j], F32).astype(BF16)
            target[there] = source[there] * keep


def stage(tree, mask, sub_rhs, diag_inverse, factor):
    levels, rhs_count, depth = sub_rhs.shape[1:]
    later = levels - 1
    cols = diag_inverse.shape[2]

    def body(
        tree_ref, mask_ref, rhs_hbm, inverse_hbm, factor_hbm, out_ref, inverse_ref, rhs_ref, landed, sems, other_sems
    ):
        blocks = factor_hbm.shape[0]
        copies = [
            pltpu.make_async_copy(factor_hbm.at[block], landed.at[block], sems.at[block])
            for block in range(blocks)
        ]
        others = [
            pltpu.make_async_copy(inverse_hbm.at[pl.ds(1, later)], inverse_ref, other_sems.at[0]),
            pltpu.make_async_copy(
                rhs_hbm.at[tree_ref[0], pl.ds(1, later)], rhs_ref, other_sems.at[1]
            ),
        ]
        for copy in copies + others:
            copy.start()
        for block, copy in enumerate(copies):
            copy.wait()
            mask_tiles(mask_ref, block, landed, out_ref)
        for copy in others:
            copy.wait()

    return call(
        body,
        [
            (factor.shape, BF16),
            ((later, depth, cols), BF16),
            ((later, rhs_count, depth), F32),
        ],
        (tree, mask, sub_rhs, diag_inverse, factor),
        [SCALARS, SCALARS, IN_PLACE, IN_PLACE, IN_PLACE],
        [
            pltpu.VMEM(factor.shape, BF16),
            pltpu.SemaphoreType.DMA((factor.shape[0],)),
            pltpu.SemaphoreType.DMA((2,)),
        ],
        "stage",
    )


def masked(mask, factor):
    def body(mask_ref, factor_ref, out_ref):
        for block in range(factor.shape[0]):
            mask_tiles(mask_ref, block, factor_ref, out_ref)

    return call(
        body, [(factor.shape, BF16)], (mask, factor), [SCALARS, ON_CHIP], name="masked"
    )[0]


def stacked(parts):
    levels, count = len(parts), len(parts[0])
    rows, cols = parts[0][0].shape

    def body(*refs):
        *part_refs, out_hbm, sems = refs
        copies = [
            pltpu.make_async_copy(
                ref, out_hbm.at[k // count, pl.ds(k % count * rows, rows)], sems.at[k]
            )
            for k, ref in enumerate(part_refs)
        ]
        for copy in copies:
            copy.start()
        for copy in copies:
            copy.wait()

    args = [pltpu.with_memory_space_constraint(part, pltpu.VMEM) for one in parts for part in one]
    return pl.pallas_call(
        body,
        out_shape=jax.ShapeDtypeStruct((levels, count * rows, cols), F32),
        in_specs=[ON_CHIP] * len(args),
        out_specs=IN_PLACE,
        scratch_shapes=[pltpu.SemaphoreType.DMA((len(args),))],
        compiler_params=pltpu.CompilerParams(vmem_limit_bytes=SCOPED_BYTES),
        name="stacked",
    )(*args)


def kept_update(halves, factor, block, before, parts=1, last=False):
    rows, cols = halves[0].shape
    out_cols = factor.shape[2]
    few = rows // parts
    places = [slice(k * few, (k + 1) * few) for k in range(parts)]

    def body(one_ref, other_ref, factor_ref, *refs):
        before_refs, outs = refs[: len(before)], refs[len(before) :]
        solved = one_ref[...] + other_ref[...]
        kept = solved.astype(BF16)
        update = product(kept, factor_ref[block])
        for ref in before_refs:
            update = update + ref[...]
        for k, whole in enumerate((update, solved, kept)):
            for ref, place in zip(outs[k * parts : (k + 1) * parts], places):
                ref[...] = whole[place]

    kinds = [((few, out_cols), F32), ((few, cols), F32), ((few, cols), BF16)]
    outs = [kind for kind in kinds[: 2 if last else 3] for _ in range(parts)]
    return call(body, outs, (*halves, factor, *before), name="kept_update")


def early_update(kept, factor, blocks):
    def body(*refs):
        *kept_refs, factor_ref, out_ref = refs
        update = product(kept_refs[0][...], factor_ref[blocks[0]])
        for ref, block in zip(kept_refs[1:], blocks[1:]):
            update = update + product(ref[...], factor_ref[block])
        out_ref[...] = update

    shape = (kept[0].shape[0], factor.shape[2])
    return call(body, [(shape, F32)], (*kept, factor), name="early_update")[0]


def root_part(rhs_rows, update_parts, root_inverse):
    def body(rhs_ref, one_ref, other_ref, inverse_ref, out_ref):
        residual = rhs_ref[...] - (one_ref[...] + other_ref[...])
        out_ref[...] = product(residual.astype(BF16), inverse_ref[...])

    shape = (rhs_rows.shape[0], root_inverse.shape[1])
    return call(
        body, [(shape, F32)], (rhs_rows, *update_parts, root_inverse), name="root_part"
    )[0]


def prow_halves(partial_sum):
    pair = partial_sum + partner(partial_sum, "core")
    return pair, partner(pair, "xl")


def owner_sums(partial_sum):
    pair = partial_sum + partner(partial_sum, PCOL, 4)
    return [pair] + [partner(pair, PCOL, bit) for bit in (2, 3, 1)]


def shards(
    sub_rhs, root_rhs, diag_inverse, root_inverse, inner_factor, inner_mask, root_factor, root_mask
):
    out_cols = inner_factor.shape[2]
    rhs_count = root_rhs.shape[0]
    tiles = out_cols // TILE
    owners = lax.axis_size(PCOL) * lax.axis_size("grid") // SUBTREES
    tree = lax.axis_index(PCOL) // owners
    first_tile = lax.axis_index(PROW) * tiles
    inner_tiles = lax.dynamic_slice_in_dim(inner_mask, first_tile, tiles, 2)
    root_tiles = lax.dynamic_slice_in_dim(root_mask, first_tile, tiles, 2)
    tree = tree.reshape(1)

    halves = prow_halves(first_solve(tree, sub_rhs, diag_inverse))
    inner, inverse, rhs = stage(tree, inner_tiles, sub_rhs, diag_inverse, inner_factor)
    root = masked(root_tiles, root_factor)
    solved, locals_ = [], []
    outs = kept_update(halves, inner, 0, (), PARTS)
    for part in range(PARTS):
        update, solved0, kept0 = outs[part::PARTS]
        halves = prow_halves(next_solve(0, part, rhs, owner_sums(update), inverse))
        early = early_update((kept0,), inner, (1,))
        update, solved1, kept1 = kept_update(halves, inner, 2, (early,))
        halves = prow_halves(next_solve(1, part, rhs, owner_sums(update), inverse))
        early = early_update((kept0, kept1), root, (0, 1))
        root_local, solved2 = kept_update(halves, root, 2, (early,), last=True)
        solved.append((solved0, solved1, solved2))
        locals_.append(root_local)
    root_local = jnp.concatenate(locals_)

    few = rhs_count // lax.axis_size(PCOL)
    first_row, first, root_local = lax.optimization_barrier(
        (lax.axis_index(PCOL) * few, lax.axis_index("core") == 0, root_local)
    )
    own_rows = lax.all_to_all(
        root_local.reshape(-1, few, out_cols), PCOL, 0, 0, tiled=True
    ).sum(axis=0)
    rhs_rows = lax.dynamic_slice(
        root_rhs, (first_row, 0), (few, out_cols), allow_negative_indices=False
    )
    sub_solution, across, rhs_rows = lax.optimization_barrier(
        (stacked(list(zip(*solved))), partner(own_rows, "grid"), rhs_rows)
    )
    part = root_part(rhs_rows, (own_rows, across), root_inverse)
    half = part.shape[1] // 2
    low, high = part[:, :half], part[:, half:]
    mine = jnp.where(first, low, high) + partner(jnp.where(first, high, low), "core")
    mine = mine + partner(mine, "xl")
    columns = to_everyone(mine, PCOL).reshape(rhs_count, half)
    others = partner(columns, "core")
    root_solution = jnp.concatenate(
        [jnp.where(first, columns, others), jnp.where(first, others, columns)], axis=1
    )
    return (sub_solution, root_solution)


def solution(mesh):
    cores = 2
    fine = Mesh(
        mesh.devices.reshape(
            mesh.shape["grid"], mesh.shape["prow"] // cores, cores, mesh.shape["pcol"]
        ),
        ("grid", "xl", "core", PCOL),
    )
    columns = ("grid", PCOL)
    return jax.shard_map(
        shards,
        mesh=fine,
        in_specs=(
            P("grid", None, None, PROW),
            P(None, PROW),
            P(None, PROW, columns),
            P(PROW, "grid"),
            P(None, columns, PROW),
            P(None, columns, None),
            P(None, columns, PROW),
            P(None, columns, None),
        ),
        out_specs=(P(None, None, columns), P(None, "grid")),
        check_vma=False,
    )
```

```python
import jax
import jax.numpy as jnp
from jax import lax
from jax.experimental import pallas as pl
from jax.experimental.pallas import tpu as pltpu
from jax.sharding import Mesh
from jax.sharding import PartitionSpec as P

LEVELS = 3
TILE = 128
PARTS = 2
PROW = ("xl", "core")
OWN = "own"
SCOPED_BYTES = 4 << 20
F32 = jnp.float32
BF16 = jnp.bfloat16

ON_CHIP = pl.BlockSpec(memory_space=pltpu.VMEM)
SCALARS = pl.BlockSpec(memory_space=pltpu.SMEM)
IN_PLACE = pl.BlockSpec(memory_space=pltpu.HBM)


def partner(shard, axis, bit=1):
    return lax.ppermute(shard, axis, [(i, i ^ bit) for i in range(lax.axis_size(axis))])


def swap_blocks(blocks):
    order = list(range(lax.axis_size(OWN)))[::-1]
    return lax.all_to_all(blocks, OWN, 0, 0, axis_index_groups=[order], tiled=True)


def to_everyone(shard):
    count = lax.axis_size(OWN)
    return swap_blocks(jnp.broadcast_to(shard[None], (count, *shard.shape)))


def call(body, outs, args, specs=None, scratch=(), name=None):
    specs = specs or [ON_CHIP] * len(args)
    args = [
        arg if spec is SCALARS else pltpu.with_memory_space_constraint(arg, spec.memory_space)
        for arg, spec in zip(args, specs)
    ]
    return pl.pallas_call(
        body,
        out_shape=[pltpu.VMEM(shape, kind) for shape, kind in outs],
        in_specs=specs,
        out_specs=[ON_CHIP] * len(outs),
        scratch_shapes=list(scratch),
        compiler_params=pltpu.CompilerParams(vmem_limit_bytes=SCOPED_BYTES),
        name=name,
    )(*args)


def product(left, right):
    return jnp.dot(left, right, preferred_element_type=F32)


def first_solve(tree, sub_rhs, diag_inverse):
    rhs_count, depth = sub_rhs.shape[2:]
    cols = diag_inverse.shape[2]
    pieces = 3
    step = depth // pieces

    def body(tree_ref, rhs_hbm, inverse_hbm, out_ref, rhs, inverse, rhs_sem, inverse_sem):
        rhs_copy = pltpu.make_async_copy(rhs_hbm.at[tree_ref[0], 0], rhs, rhs_sem)
        rhs_copy.start()
        copies = []
        for piece in range(pieces):
            part = pl.ds(piece * step, step)
            copies.append(
                pltpu.make_async_copy(
                    inverse_hbm.at[0, part], inverse.at[part], inverse_sem.at[piece]
                )
            )
            copies[-1].start()
        rhs_copy.wait()
        total = jnp.zeros((rhs_count, cols), F32)
        for piece in range(pieces):
            copies[piece].wait()
            part = slice(piece * step, (piece + 1) * step)
            total = total + product(rhs[:, part].astype(BF16), inverse[part, :])
        out_ref[...] = total

    return call(
        body,
        [((rhs_count, cols), F32)],
        (tree, sub_rhs, diag_inverse),
        [SCALARS, IN_PLACE, IN_PLACE],
        [
            pltpu.VMEM((rhs_count, depth), F32),
            pltpu.VMEM((depth, cols), BF16),
            pltpu.SemaphoreType.DMA,
            pltpu.SemaphoreType.DMA((pieces,)),
        ],
        "first_solve",
    )[0]


def next_solve(place, part, rhs, sums, diag_inverse):
    few = sums[0].shape[0]
    rows = slice(part * few, (part + 1) * few)

    def body(rhs_ref, *refs):
        *sum_refs, inverse_ref, out_ref = refs
        update = sum_refs[0][...]
        for ref in sum_refs[1:]:
            update = update + ref[...]
        residual = (rhs_ref[place, rows] - update).astype(BF16)
        out_ref[...] = product(residual, inverse_ref[place])

    shape = (few, diag_inverse.shape[2])
    return call(body, [(shape, F32)], (rhs, *sums, diag_inverse), name="next_solve")[0]


def mask_tiles(mask_ref, block, source, target):
    rows, cols = source.shape[1:]
    for i in range(rows // TILE):
        for j in range(cols // TILE):
            there = (
                block,
                slice(i * TILE, (i + 1) * TILE),
                slice(j * TILE, (j + 1) * TILE),
            )
            keep = jnp.full((TILE, TILE), mask_ref[block, i, j], F32).astype(BF16)
            target[there] = source[there] * keep


def stage(tree, mask, sub_rhs, diag_inverse, factor):
    levels, rhs_count, depth = sub_rhs.shape[1:]
    later = levels - 1
    cols = diag_inverse.shape[2]

    def body(
        tree_ref, mask_ref, rhs_hbm, inverse_hbm, factor_hbm, out_ref, inverse_ref, rhs_ref, landed, sems, other_sems
    ):
        blocks = factor_hbm.shape[0]
        copies = [
            pltpu.make_async_copy(factor_hbm.at[block], landed.at[block], sems.at[block])
            for block in range(blocks)
        ]
        others = [
            pltpu.make_async_copy(inverse_hbm.at[pl.ds(1, later)], inverse_ref, other_sems.at[0]),
            pltpu.make_async_copy(
                rhs_hbm.at[tree_ref[0], pl.ds(1, later)], rhs_ref, other_sems.at[1]
            ),
        ]
        for copy in copies + others:
            copy.start()
        for block, copy in enumerate(copies):
            copy.wait()
            mask_tiles(mask_ref, block, landed, out_ref)
        for copy in others:
            copy.wait()

    return call(
        body,
        [
            (factor.shape, BF16),
            ((later, depth, cols), BF16),
            ((later, rhs_count, depth), F32),
        ],
        (tree, mask, sub_rhs, diag_inverse, factor),
        [SCALARS, SCALARS, IN_PLACE, IN_PLACE, IN_PLACE],
        [
            pltpu.VMEM(factor.shape, BF16),
            pltpu.SemaphoreType.DMA((factor.shape[0],)),
            pltpu.SemaphoreType.DMA((2,)),
        ],
        "stage",
    )


def masked(mask, factor):
    def body(mask_ref, factor_ref, out_ref):
        for block in range(factor.shape[0]):
            mask_tiles(mask_ref, block, factor_ref, out_ref)

    return call(
        body, [(factor.shape, BF16)], (mask, factor), [SCALARS, ON_CHIP], name="masked"
    )[0]


def stacked(parts):
    levels, count = len(parts), len(parts[0])
    rows, cols = parts[0][0].shape

    def body(*refs):
        *part_refs, out_hbm, sems = refs
        copies = [
            pltpu.make_async_copy(
                ref, out_hbm.at[k // count, pl.ds(k % count * rows, rows)], sems.at[k]
            )
            for k, ref in enumerate(part_refs)
        ]
        for copy in copies:
            copy.start()
        for copy in copies:
            copy.wait()

    args = [pltpu.with_memory_space_constraint(part, pltpu.VMEM) for one in parts for part in one]
    return pl.pallas_call(
        body,
        out_shape=jax.ShapeDtypeStruct((levels, count * rows, cols), F32),
        in_specs=[ON_CHIP] * len(args),
        out_specs=IN_PLACE,
        scratch_shapes=[pltpu.SemaphoreType.DMA((len(args),))],
        compiler_params=pltpu.CompilerParams(vmem_limit_bytes=SCOPED_BYTES),
        name="stacked",
    )(*args)


def kept_update(halves, factor, block, before, parts=1, last=False):
    rows, cols = halves[0].shape
    out_cols = factor.shape[2]
    few = rows // parts
    places = [slice(k * few, (k + 1) * few) for k in range(parts)]

    def body(one_ref, other_ref, factor_ref, *refs):
        before_refs, outs = refs[: len(before)], refs[len(before) :]
        solved = one_ref[...] + other_ref[...]
        kept = solved.astype(BF16)
        update = product(kept, factor_ref[block])
        for ref in before_refs:
            update = update + ref[...]
        for k, whole in enumerate((update, solved, kept)):
            for ref, place in zip(outs[k * parts : (k + 1) * parts], places):
                ref[...] = whole[place]

    kinds = [((few, out_cols), F32), ((few, cols), F32), ((few, cols), BF16)]
    outs = [kind for kind in kinds[: 2 if last else 3] for _ in range(parts)]
    return call(body, outs, (*halves, factor, *before), name="kept_update")


def early_update(kept, factor, blocks):
    def body(*refs):
        *kept_refs, factor_ref, out_ref = refs
        update = product(kept_refs[0][...], factor_ref[blocks[0]])
        for ref, block in zip(kept_refs[1:], blocks[1:]):
            update = update + product(ref[...], factor_ref[block])
        out_ref[...] = update

    shape = (kept[0].shape[0], factor.shape[2])
    return call(body, [(shape, F32)], (*kept, factor), name="early_update")[0]


def root_part(rhs_rows, update_parts, root_inverse):
    def body(rhs_ref, one_ref, other_ref, inverse_ref, out_ref):
        residual = rhs_ref[...] - (one_ref[...] + other_ref[...])
        out_ref[...] = product(residual.astype(BF16), inverse_ref[...])

    shape = (rhs_rows.shape[0], root_inverse.shape[1])
    return call(
        body, [(shape, F32)], (rhs_rows, *update_parts, root_inverse), name="root_part"
    )[0]


def prow_halves(partial_sum):
    pair = partial_sum + partner(partial_sum, "core")
    return pair, partner(pair, "xl")


def owner_sums(partial_sum):
    far, back, near = [partner(partial_sum, OWN, bit) for bit in (2, 3, 1)]
    line = (partial_sum + near) + (far + back)
    return [line, partner(line, OWN, 4)]


def shards(
    sub_rhs, root_rhs, diag_inverse, root_inverse, inner_factor, inner_mask, root_factor, root_mask
):
    out_cols = inner_factor.shape[2]
    rhs_count = root_rhs.shape[0]
    tiles = out_cols // TILE
    tree = lax.axis_index("zt")
    first_tile = lax.axis_index(PROW) * tiles
    inner_tiles = lax.dynamic_slice_in_dim(inner_mask, first_tile, tiles, 2)
    root_tiles = lax.dynamic_slice_in_dim(root_mask, first_tile, tiles, 2)
    tree = tree.reshape(1)

    halves = prow_halves(first_solve(tree, sub_rhs, diag_inverse))
    inner, inverse, rhs = stage(tree, inner_tiles, sub_rhs, diag_inverse, inner_factor)
    root = masked(root_tiles, root_factor)
    solved, locals_ = [], []
    outs = kept_update(halves, inner, 0, (), PARTS)
    for part in range(PARTS):
        update, solved0, kept0 = outs[part::PARTS]
        halves = prow_halves(next_solve(0, part, rhs, owner_sums(update), inverse))
        early = early_update((kept0,), inner, (1,))
        update, solved1, kept1 = kept_update(halves, inner, 2, (early,))
        halves = prow_halves(next_solve(1, part, rhs, owner_sums(update), inverse))
        early = early_update((kept0, kept1), root, (0, 1))
        root_local, solved2 = kept_update(halves, root, 2, (early,), last=True)
        solved.append((solved0, solved1, solved2))
        locals_.append(root_local)
    root_local = jnp.concatenate(locals_)

    owners = lax.axis_size(OWN)
    few = rhs_count // owners
    place = owners - 1 - lax.axis_index(OWN)
    own_rows = swap_blocks(root_local.reshape(owners, few, out_cols)).sum(axis=0)
    sub_solution, across = lax.optimization_barrier(
        (stacked(list(zip(*solved))), partner(own_rows, "grid"))
    )
    total = own_rows + across
    total = total + partner(total, "zt", 1)
    rhs_rows = lax.dynamic_slice_in_dim(root_rhs, place * few, few, 0)
    part = root_part(rhs_rows, (total, partner(total, "zt", 3)), root_inverse)
    pair, other = prow_halves(part)
    root_solution = to_everyone(pair + other).reshape(rhs_count, part.shape[1])
    return (sub_solution, root_solution)


def solution(mesh):
    prow, pcol = mesh.shape["prow"], mesh.shape["pcol"]
    cores = 2
    trees = 8 // mesh.shape["grid"]
    fine = Mesh(
        mesh.devices.reshape(
            mesh.shape["grid"], prow // cores, cores, trees, pcol // trees
        ),
        ("grid", "xl", "core", "zt", "own"),
    )
    columns = ("grid", "zt", "own")
    return jax.shard_map(
        shards,
        mesh=fine,
        in_specs=(
            P("grid", None, None, PROW),
            P(None, PROW),
            P(None, PROW, columns),
            P(PROW, "grid"),
            P(None, columns, PROW),
            P(None, columns, None),
            P(None, columns, PROW),
            P(None, columns, None),
        ),
        out_specs=(P(None, None, columns), P(None, "grid")),
        check_vma=False,
    )
```

```python
import jax
import jax.numpy as jnp
from jax import lax
from jax.experimental import pallas as pl
from jax.experimental.pallas import tpu as pltpu
from jax.sharding import Mesh
from jax.sharding import PartitionSpec as P

LEVELS = 3
TILE = 128
PARTS = 2
PROW = ("xl", "core")
OWN = "own"
SCOPED_BYTES = 4 << 20
F32 = jnp.float32
BF16 = jnp.bfloat16

ON_CHIP = pl.BlockSpec(memory_space=pltpu.VMEM)
SCALARS = pl.BlockSpec(memory_space=pltpu.SMEM)
IN_PLACE = pl.BlockSpec(memory_space=pltpu.HBM)


def partner(shard, axis, bit=1):
    return lax.ppermute(shard, axis, [(i, i ^ bit) for i in range(lax.axis_size(axis))])


def swap_blocks(blocks):
    order = list(range(lax.axis_size(OWN)))[::-1]
    return lax.all_to_all(blocks, OWN, 0, 0, axis_index_groups=[order], tiled=True)


def to_everyone(shard):
    count = lax.axis_size(OWN)
    return swap_blocks(jnp.broadcast_to(shard[None], (count, *shard.shape)))


def call(body, outs, args, specs=None, scratch=(), name=None):
    specs = specs or [ON_CHIP] * len(args)
    args = [
        arg if spec is SCALARS else pltpu.with_memory_space_constraint(arg, spec.memory_space)
        for arg, spec in zip(args, specs)
    ]
    return pl.pallas_call(
        body,
        out_shape=[pltpu.VMEM(shape, kind) for shape, kind in outs],
        in_specs=specs,
        out_specs=[ON_CHIP] * len(outs),
        scratch_shapes=list(scratch),
        compiler_params=pltpu.CompilerParams(vmem_limit_bytes=SCOPED_BYTES),
        name=name,
    )(*args)


def product(left, right):
    return jnp.dot(left, right, preferred_element_type=F32)


def first_solve(tree, sub_rhs, diag_inverse):
    rhs_count, depth = sub_rhs.shape[2:]
    cols = diag_inverse.shape[2]
    pieces = 3
    step = depth // pieces

    def body(tree_ref, rhs_hbm, inverse_hbm, out_ref, rhs, inverse, rhs_sem, inverse_sem):
        rhs_copy = pltpu.make_async_copy(rhs_hbm.at[tree_ref[0], 0], rhs, rhs_sem)
        rhs_copy.start()
        copies = []
        for piece in range(pieces):
            part = pl.ds(piece * step, step)
            copies.append(
                pltpu.make_async_copy(
                    inverse_hbm.at[0, part], inverse.at[part], inverse_sem.at[piece]
                )
            )
            copies[-1].start()
        rhs_copy.wait()
        total = jnp.zeros((rhs_count, cols), F32)
        for piece in range(pieces):
            copies[piece].wait()
            part = slice(piece * step, (piece + 1) * step)
            total = total + product(rhs[:, part].astype(BF16), inverse[part, :])
        out_ref[...] = total

    return call(
        body,
        [((rhs_count, cols), F32)],
        (tree, sub_rhs, diag_inverse),
        [SCALARS, IN_PLACE, IN_PLACE],
        [
            pltpu.VMEM((rhs_count, depth), F32),
            pltpu.VMEM((depth, cols), BF16),
            pltpu.SemaphoreType.DMA,
            pltpu.SemaphoreType.DMA((pieces,)),
        ],
        "first_solve",
    )[0]


def next_solve(place, part, rhs, sums, diag_inverse):
    few = sums[0].shape[0]
    rows = slice(part * few, (part + 1) * few)

    def body(rhs_ref, *refs):
        *sum_refs, inverse_ref, out_ref = refs
        update = sum_refs[0][...]
        for ref in sum_refs[1:]:
            update = update + ref[...]
        residual = (rhs_ref[place, rows] - update).astype(BF16)
        out_ref[...] = product(residual, inverse_ref[place])

    shape = (few, diag_inverse.shape[2])
    return call(body, [(shape, F32)], (rhs, *sums, diag_inverse), name="next_solve")[0]


def mask_tiles(mask_ref, block, source, target):
    rows, cols = source.shape[1:]
    for i in range(rows // TILE):
        for j in range(cols // TILE):
            there = (
                block,
                slice(i * TILE, (i + 1) * TILE),
                slice(j * TILE, (j + 1) * TILE),
            )
            keep = jnp.full((TILE, TILE), mask_ref[block, i, j], F32).astype(BF16)
            target[there] = source[there] * keep


def stage(tree, mask, sub_rhs, diag_inverse, factor):
    levels, rhs_count, depth = sub_rhs.shape[1:]
    later = levels - 1
    cols = diag_inverse.shape[2]

    def body(
        tree_ref, mask_ref, rhs_hbm, inverse_hbm, factor_hbm, out_ref, inverse_ref, rhs_ref, landed, sems, other_sems
    ):
        blocks = factor_hbm.shape[0]
        copies = [
            pltpu.make_async_copy(factor_hbm.at[block], landed.at[block], sems.at[block])
            for block in range(blocks)
        ]
        others = [
            pltpu.make_async_copy(inverse_hbm.at[pl.ds(1, later)], inverse_ref, other_sems.at[0]),
            pltpu.make_async_copy(
                rhs_hbm.at[tree_ref[0], pl.ds(1, later)], rhs_ref, other_sems.at[1]
            ),
        ]
        for copy in copies + others:
            copy.start()
        for block, copy in enumerate(copies):
            copy.wait()
            mask_tiles(mask_ref, block, landed, out_ref)
        for copy in others:
            copy.wait()

    return call(
        body,
        [
            (factor.shape, BF16),
            ((later, depth, cols), BF16),
            ((later, rhs_count, depth), F32),
        ],
        (tree, mask, sub_rhs, diag_inverse, factor),
        [SCALARS, SCALARS, IN_PLACE, IN_PLACE, IN_PLACE],
        [
            pltpu.VMEM(factor.shape, BF16),
            pltpu.SemaphoreType.DMA((factor.shape[0],)),
            pltpu.SemaphoreType.DMA((2,)),
        ],
        "stage",
    )


def masked(mask, factor):
    def body(mask_ref, factor_ref, out_ref):
        for block in range(factor.shape[0]):
            mask_tiles(mask_ref, block, factor_ref, out_ref)

    return call(
        body, [(factor.shape, BF16)], (mask, factor), [SCALARS, ON_CHIP], name="masked"
    )[0]


def stacked(parts):
    levels, count = len(parts), len(parts[0])
    rows, cols = parts[0][0].shape

    def body(*refs):
        *part_refs, out_hbm, sems = refs
        copies = [
            pltpu.make_async_copy(
                ref, out_hbm.at[k // count, pl.ds(k % count * rows, rows)], sems.at[k]
            )
            for k, ref in enumerate(part_refs)
        ]
        for copy in copies:
            copy.start()
        for copy in copies:
            copy.wait()

    args = [pltpu.with_memory_space_constraint(part, pltpu.VMEM) for one in parts for part in one]
    return pl.pallas_call(
        body,
        out_shape=jax.ShapeDtypeStruct((levels, count * rows, cols), F32),
        in_specs=[ON_CHIP] * len(args),
        out_specs=IN_PLACE,
        scratch_shapes=[pltpu.SemaphoreType.DMA((len(args),))],
        compiler_params=pltpu.CompilerParams(vmem_limit_bytes=SCOPED_BYTES),
        name="stacked",
    )(*args)


def kept_update(halves, factor, block, before, parts=1, last=False):
    rows, cols = halves[0].shape
    out_cols = factor.shape[2]
    few = rows // parts
    places = [slice(k * few, (k + 1) * few) for k in range(parts)]

    def body(one_ref, other_ref, factor_ref, *refs):
        before_refs, outs = refs[: len(before)], refs[len(before) :]
        solved = one_ref[...] + other_ref[...]
        kept = solved.astype(BF16)
        update = product(kept, factor_ref[block])
        for ref in before_refs:
            update = update + ref[...]
        for k, whole in enumerate((update, solved, kept)):
            for ref, place in zip(outs[k * parts : (k + 1) * parts], places):
                ref[...] = whole[place]

    kinds = [((few, out_cols), F32), ((few, cols), F32), ((few, cols), BF16)]
    outs = [kind for kind in kinds[: 2 if last else 3] for _ in range(parts)]
    return call(body, outs, (*halves, factor, *before), name="kept_update")


def early_update(kept, factor, blocks):
    def body(*refs):
        *kept_refs, factor_ref, out_ref = refs
        update = product(kept_refs[0][...], factor_ref[blocks[0]])
        for ref, block in zip(kept_refs[1:], blocks[1:]):
            update = update + product(ref[...], factor_ref[block])
        out_ref[...] = update

    shape = (kept[0].shape[0], factor.shape[2])
    return call(body, [(shape, F32)], (*kept, factor), name="early_update")[0]


def root_part(rhs_rows, update_parts, root_inverse):
    def body(rhs_ref, one_ref, other_ref, inverse_ref, out_ref):
        residual = rhs_ref[...] - (one_ref[...] + other_ref[...])
        out_ref[...] = product(residual.astype(BF16), inverse_ref[...])

    shape = (rhs_rows.shape[0], root_inverse.shape[1])
    return call(
        body, [(shape, F32)], (rhs_rows, *update_parts, root_inverse), name="root_part"
    )[0]


def prow_halves(partial_sum):
    pair = partial_sum + partner(partial_sum, "core")
    return pair, partner(pair, "xl")


def owner_sums(partial_sum, part):
    if part % 2 == 0:
        pair = partial_sum + partner(partial_sum, OWN, 4)
        return [pair] + [partner(pair, OWN, bit) for bit in (2, 3, 1)]
    far, back, near = [partner(partial_sum, OWN, bit) for bit in (2, 3, 1)]
    line = (partial_sum + near) + (far + back)
    return [line, partner(line, OWN, 4)]


def shards(
    sub_rhs, root_rhs, diag_inverse, root_inverse, inner_factor, inner_mask, root_factor, root_mask
):
    out_cols = inner_factor.shape[2]
    rhs_count = root_rhs.shape[0]
    tiles = out_cols // TILE
    tree = lax.axis_index("zt")
    first_tile = lax.axis_index(PROW) * tiles
    inner_tiles = lax.dynamic_slice_in_dim(inner_mask, first_tile, tiles, 2)
    root_tiles = lax.dynamic_slice_in_dim(root_mask, first_tile, tiles, 2)
    tree = tree.reshape(1)

    halves = prow_halves(first_solve(tree, sub_rhs, diag_inverse))
    inner, inverse, rhs = stage(tree, inner_tiles, sub_rhs, diag_inverse, inner_factor)
    root = masked(root_tiles, root_factor)
    solved, locals_ = [], []
    outs = kept_update(halves, inner, 0, (), PARTS)
    for part in range(PARTS):
        update, solved0, kept0 = outs[part::PARTS]
        halves = prow_halves(next_solve(0, part, rhs, owner_sums(update, part), inverse))
        early = early_update((kept0,), inner, (1,))
        update, solved1, kept1 = kept_update(halves, inner, 2, (early,))
        halves = prow_halves(next_solve(1, part, rhs, owner_sums(update, part), inverse))
        early = early_update((kept0, kept1), root, (0, 1))
        root_local, solved2 = kept_update(halves, root, 2, (early,), last=True)
        solved.append((solved0, solved1, solved2))
        locals_.append(root_local)
    root_local = jnp.concatenate(locals_)

    owners = lax.axis_size(OWN)
    few = rhs_count // owners
    place = owners - 1 - lax.axis_index(OWN)
    own_rows = swap_blocks(root_local.reshape(owners, few, out_cols)).sum(axis=0)
    sub_solution, across = lax.optimization_barrier(
        (stacked(list(zip(*solved))), partner(own_rows, "grid"))
    )
    total = own_rows + across
    total = total + partner(total, "zt", 1)
    rhs_rows = lax.dynamic_slice_in_dim(root_rhs, place * few, few, 0)
    part = root_part(rhs_rows, (total, partner(total, "zt", 3)), root_inverse)
    pair, other = prow_halves(part)
    root_solution = to_everyone(pair + other).reshape(rhs_count, part.shape[1])
    return (sub_solution, root_solution)


def solution(mesh):
    prow, pcol = mesh.shape["prow"], mesh.shape["pcol"]
    cores = 2
    trees = 8 // mesh.shape["grid"]
    fine = Mesh(
        mesh.devices.reshape(
            mesh.shape["grid"], prow // cores, cores, trees, pcol // trees
        ),
        ("grid", "xl", "core", "zt", "own"),
    )
    columns = ("grid", "zt", "own")
    return jax.shard_map(
        shards,
        mesh=fine,
        in_specs=(
            P("grid", None, None, PROW),
            P(None, PROW),
            P(None, PROW, columns),
            P(PROW, "grid"),
            P(None, columns, PROW),
            P(None, columns, None),
            P(None, columns, PROW),
            P(None, columns, None),
        ),
        out_specs=(P(None, None, columns), P(None, "grid")),
        check_vma=False,
    )
```

```python
import jax
import jax.numpy as jnp
from jax import lax
from jax.experimental import pallas as pl
from jax.experimental.pallas import tpu as pltpu
from jax.sharding import Mesh
from jax.sharding import PartitionSpec as P

LEVELS = 3
TILE = 128
SPLIT = (5, 3)
PROW = ("xl", "core")
OWN = "own"
SCOPED_BYTES = 8 << 20
F32 = jnp.float32
BF16 = jnp.bfloat16

ON_CHIP = pl.BlockSpec(memory_space=pltpu.VMEM)
SCALARS = pl.BlockSpec(memory_space=pltpu.SMEM)
IN_PLACE = pl.BlockSpec(memory_space=pltpu.HBM)


def partner(shard, axis, bit=1):
    return lax.ppermute(shard, axis, [(i, i ^ bit) for i in range(lax.axis_size(axis))])


def swap_blocks(blocks):
    order = list(range(lax.axis_size(OWN)))[::-1]
    return lax.all_to_all(blocks, OWN, 0, 0, axis_index_groups=[order], tiled=True)


def to_everyone(shard):
    count = lax.axis_size(OWN)
    return swap_blocks(jnp.broadcast_to(shard[None], (count, *shard.shape)))


def call(body, outs, args, specs=None, scratch=(), name=None):
    specs = specs or [ON_CHIP] * len(args)
    args = [
        arg if spec is SCALARS else pltpu.with_memory_space_constraint(arg, spec.memory_space)
        for arg, spec in zip(args, specs)
    ]
    return pl.pallas_call(
        body,
        out_shape=[pltpu.VMEM(shape, kind) for shape, kind in outs],
        in_specs=specs,
        out_specs=[ON_CHIP] * len(outs),
        scratch_shapes=list(scratch),
        compiler_params=pltpu.CompilerParams(vmem_limit_bytes=SCOPED_BYTES),
        name=name,
    )(*args)


def places(rows):
    ends = [rows * sum(SPLIT[:k]) // sum(SPLIT) for k in range(len(SPLIT) + 1)]
    return [slice(*pair) for pair in zip(ends[:-1], ends[1:])]


def product(left, right):
    return jnp.dot(left, right, preferred_element_type=F32)


def first_solve(tree, sub_rhs, diag_inverse):
    rhs_count, depth = sub_rhs.shape[2:]
    cols = diag_inverse.shape[2]
    pieces = 3
    step = depth // pieces

    def body(tree_ref, rhs_hbm, inverse_hbm, out_ref, rhs, inverse, rhs_sem, inverse_sem):
        rhs_copy = pltpu.make_async_copy(rhs_hbm.at[tree_ref[0], 0], rhs, rhs_sem)
        rhs_copy.start()
        copies = []
        for piece in range(pieces):
            part = pl.ds(piece * step, step)
            copies.append(
                pltpu.make_async_copy(
                    inverse_hbm.at[0, part], inverse.at[part], inverse_sem.at[piece]
                )
            )
            copies[-1].start()
        rhs_copy.wait()
        total = jnp.zeros((rhs_count, cols), F32)
        for piece in range(pieces):
            copies[piece].wait()
            part = slice(piece * step, (piece + 1) * step)
            total = total + product(rhs[:, part].astype(BF16), inverse[part, :])
        out_ref[...] = total

    return call(
        body,
        [((rhs_count, cols), F32)],
        (tree, sub_rhs, diag_inverse),
        [SCALARS, IN_PLACE, IN_PLACE],
        [
            pltpu.VMEM((rhs_count, depth), F32),
            pltpu.VMEM((depth, cols), BF16),
            pltpu.SemaphoreType.DMA,
            pltpu.SemaphoreType.DMA((pieces,)),
        ],
        "first_solve",
    )[0]


def next_solve(place, part, rhs, sums, diag_inverse):
    few = sums[0].shape[0]
    rows = places(rhs.shape[1])[part]

    def body(rhs_ref, *refs):
        *sum_refs, inverse_ref, out_ref = refs
        update = sum_refs[0][...]
        for ref in sum_refs[1:]:
            update = update + ref[...]
        residual = (rhs_ref[place, rows] - update).astype(BF16)
        out_ref[...] = product(residual, inverse_ref[place])

    shape = (few, diag_inverse.shape[2])
    return call(body, [(shape, F32)], (rhs, *sums, diag_inverse), name="next_solve")[0]


def mask_tiles(mask_ref, block, source, target):
    rows, cols = source.shape[1:]
    for i in range(rows // TILE):
        for j in range(cols // TILE):
            there = (
                block,
                slice(i * TILE, (i + 1) * TILE),
                slice(j * TILE, (j + 1) * TILE),
            )
            keep = jnp.full((TILE, TILE), mask_ref[block, i, j], F32).astype(BF16)
            target[there] = source[there] * keep


def stage(tree, mask, sub_rhs, diag_inverse, factor):
    levels, rhs_count, depth = sub_rhs.shape[1:]
    later = levels - 1
    cols = diag_inverse.shape[2]

    def body(
        tree_ref, mask_ref, rhs_hbm, inverse_hbm, factor_hbm, out_ref, inverse_ref, rhs_ref, landed, sems, other_sems
    ):
        blocks = factor_hbm.shape[0]
        copies = [
            pltpu.make_async_copy(factor_hbm.at[block], landed.at[block], sems.at[block])
            for block in range(blocks)
        ]
        others = [
            pltpu.make_async_copy(inverse_hbm.at[pl.ds(1, later)], inverse_ref, other_sems.at[0]),
            pltpu.make_async_copy(
                rhs_hbm.at[tree_ref[0], pl.ds(1, later)], rhs_ref, other_sems.at[1]
            ),
        ]
        for copy in copies + others:
            copy.start()
        for block, copy in enumerate(copies):
            copy.wait()
            mask_tiles(mask_ref, block, landed, out_ref)
        for copy in others:
            copy.wait()

    return call(
        body,
        [
            (factor.shape, BF16),
            ((later, depth, cols), BF16),
            ((later, rhs_count, depth), F32),
        ],
        (tree, mask, sub_rhs, diag_inverse, factor),
        [SCALARS, SCALARS, IN_PLACE, IN_PLACE, IN_PLACE],
        [
            pltpu.VMEM(factor.shape, BF16),
            pltpu.SemaphoreType.DMA((factor.shape[0],)),
            pltpu.SemaphoreType.DMA((2,)),
        ],
        "stage",
    )


def masked(mask, factor):
    def body(mask_ref, factor_ref, out_ref):
        for block in range(factor.shape[0]):
            mask_tiles(mask_ref, block, factor_ref, out_ref)

    return call(
        body, [(factor.shape, BF16)], (mask, factor), [SCALARS, ON_CHIP], name="masked"
    )[0]


def stacked(parts):
    levels, count = len(parts), len(parts[0])
    rows = sum(part.shape[0] for part in parts[0])
    cols = parts[0][0].shape[1]
    pieces = places(rows)

    def body(*refs):
        *part_refs, out_hbm, sems = refs
        copies = [
            pltpu.make_async_copy(
                ref, out_hbm.at[k // count, pieces[k % count]], sems.at[k]
            )
            for k, ref in enumerate(part_refs)
        ]
        for copy in copies:
            copy.start()
        for copy in copies:
            copy.wait()

    args = [pltpu.with_memory_space_constraint(part, pltpu.VMEM) for one in parts for part in one]
    return pl.pallas_call(
        body,
        out_shape=jax.ShapeDtypeStruct((levels, rows, cols), F32),
        in_specs=[ON_CHIP] * len(args),
        out_specs=IN_PLACE,
        scratch_shapes=[pltpu.SemaphoreType.DMA((len(args),))],
        compiler_params=pltpu.CompilerParams(vmem_limit_bytes=SCOPED_BYTES),
        name="stacked",
    )(*args)


def kept_update(halves, factor, block, before, split=False, last=False):
    rows, cols = halves[0].shape
    out_cols = factor.shape[2]
    pieces = places(rows) if split else [slice(0, rows)]
    parts = len(pieces)

    def body(one_ref, other_ref, factor_ref, *refs):
        before_refs, outs = refs[: len(before)], refs[len(before) :]
        solved = one_ref[...] + other_ref[...]
        kept = solved.astype(BF16)
        update = product(kept, factor_ref[block])
        for ref in before_refs:
            update = update + ref[...]
        for k, whole in enumerate((update, solved, kept)):
            for ref, place in zip(outs[k * parts : (k + 1) * parts], pieces):
                ref[...] = whole[place]

    kinds = [(out_cols, F32), (cols, F32), (cols, BF16)][: 2 if last else 3]
    outs = [
        ((piece.stop - piece.start, width), kind) for width, kind in kinds for piece in pieces
    ]
    return call(body, outs, (*halves, factor, *before), name="kept_update")


def early_update(kept, factor, blocks):
    def body(*refs):
        *kept_refs, factor_ref, out_ref = refs
        update = product(kept_refs[0][...], factor_ref[blocks[0]])
        for ref, block in zip(kept_refs[1:], blocks[1:]):
            update = update + product(ref[...], factor_ref[block])
        out_ref[...] = update

    shape = (kept[0].shape[0], factor.shape[2])
    return call(body, [(shape, F32)], (*kept, factor), name="early_update")[0]


def root_part(rhs_rows, update_parts, root_inverse):
    def body(rhs_ref, one_ref, other_ref, inverse_ref, out_ref):
        residual = rhs_ref[...] - (one_ref[...] + other_ref[...])
        out_ref[...] = product(residual.astype(BF16), inverse_ref[...])

    shape = (rhs_rows.shape[0], root_inverse.shape[1])
    return call(
        body, [(shape, F32)], (rhs_rows, *update_parts, root_inverse), name="root_part"
    )[0]


def prow_halves(partial_sum):
    pair = partial_sum + partner(partial_sum, "core")
    return pair, partner(pair, "xl")


def owner_sums(partial_sum, part):
    if part % 2 == 0:
        pair = partial_sum + partner(partial_sum, OWN, 4)
        return [pair] + [partner(pair, OWN, bit) for bit in (2, 3, 1)]
    far, back, near = [partner(partial_sum, OWN, bit) for bit in (2, 3, 1)]
    line = (partial_sum + near) + (far + back)
    return [line, partner(line, OWN, 4)]


def shards(
    sub_rhs, root_rhs, diag_inverse, root_inverse, inner_factor, inner_mask, root_factor, root_mask
):
    out_cols = inner_factor.shape[2]
    rhs_count = root_rhs.shape[0]
    tiles = out_cols // TILE
    tree = lax.axis_index("zt")
    first_tile = lax.axis_index(PROW) * tiles
    inner_tiles = lax.dynamic_slice_in_dim(inner_mask, first_tile, tiles, 2)
    root_tiles = lax.dynamic_slice_in_dim(root_mask, first_tile, tiles, 2)
    tree = tree.reshape(1)

    halves = prow_halves(first_solve(tree, sub_rhs, diag_inverse))
    inner, inverse, rhs = stage(tree, inner_tiles, sub_rhs, diag_inverse, inner_factor)
    root = masked(root_tiles, root_factor)
    solved, locals_ = [], []
    outs = kept_update(halves, inner, 0, (), split=True)
    for part in range(len(SPLIT)):
        update, solved0, kept0 = outs[part :: len(SPLIT)]
        halves = prow_halves(next_solve(0, part, rhs, owner_sums(update, part), inverse))
        early = early_update((kept0,), inner, (1,))
        update, solved1, kept1 = kept_update(halves, inner, 2, (early,))
        halves = prow_halves(next_solve(1, part, rhs, owner_sums(update, part), inverse))
        early = early_update((kept0, kept1), root, (0, 1))
        root_local, solved2 = kept_update(halves, root, 2, (early,), last=True)
        solved.append((solved0, solved1, solved2))
        locals_.append(root_local)
    root_local = jnp.concatenate(locals_)

    owners = lax.axis_size(OWN)
    few = rhs_count // owners
    place = owners - 1 - lax.axis_index(OWN)
    own_rows = swap_blocks(root_local.reshape(owners, few, out_cols)).sum(axis=0)
    sub_solution, across = lax.optimization_barrier(
        (stacked(list(zip(*solved))), partner(own_rows, "grid"))
    )
    total = own_rows + across
    total = total + partner(total, "zt", 1)
    rhs_rows = lax.dynamic_slice_in_dim(root_rhs, place * few, few, 0)
    part = root_part(rhs_rows, (total, partner(total, "zt", 3)), root_inverse)
    pair, other = prow_halves(part)
    root_solution = to_everyone(pair + other).reshape(rhs_count, part.shape[1])
    return (sub_solution, root_solution)


def solution(mesh):
    prow, pcol = mesh.shape["prow"], mesh.shape["pcol"]
    cores = 2
    trees = 8 // mesh.shape["grid"]
    fine = Mesh(
        mesh.devices.reshape(
            mesh.shape["grid"], prow // cores, cores, trees, pcol // trees
        ),
        ("grid", "xl", "core", "zt", "own"),
    )
    columns = ("grid", "zt", "own")
    return jax.shard_map(
        shards,
        mesh=fine,
        in_specs=(
            P("grid", None, None, PROW),
            P(None, PROW),
            P(None, PROW, columns),
            P(PROW, "grid"),
            P(None, columns, PROW),
            P(None, columns, None),
            P(None, columns, PROW),
            P(None, columns, None),
        ),
        out_specs=(P(None, None, columns), P(None, "grid")),
        check_vma=False,
    )
```

```python
import jax
import jax.numpy as jnp
from jax import lax
from jax.experimental import pallas as pl
from jax.experimental.pallas import tpu as pltpu
from jax.sharding import Mesh
from jax.sharding import PartitionSpec as P

LEVELS = 3
TILE = 128
PARTS = 2
PROW = ("xl", "core")
OWN = "own"
SCOPED_BYTES = 4 << 20
F32 = jnp.float32
BF16 = jnp.bfloat16

ON_CHIP = pl.BlockSpec(memory_space=pltpu.VMEM)
SCALARS = pl.BlockSpec(memory_space=pltpu.SMEM)
IN_PLACE = pl.BlockSpec(memory_space=pltpu.HBM)


def partner(shard, axis, bit=1):
    return lax.ppermute(shard, axis, [(i, i ^ bit) for i in range(lax.axis_size(axis))])


def swap_blocks(blocks):
    order = list(range(lax.axis_size(OWN)))[::-1]
    return lax.all_to_all(blocks, OWN, 0, 0, axis_index_groups=[order], tiled=True)


def to_everyone(shard):
    count = lax.axis_size(OWN)
    return swap_blocks(jnp.broadcast_to(shard[None], (count, *shard.shape)))


def call(body, outs, args, specs=None, scratch=(), name=None):
    specs = specs or [ON_CHIP] * len(args)
    args = [
        arg if spec is SCALARS else pltpu.with_memory_space_constraint(arg, spec.memory_space)
        for arg, spec in zip(args, specs)
    ]
    return pl.pallas_call(
        body,
        out_shape=[pltpu.VMEM(shape, kind) for shape, kind in outs],
        in_specs=specs,
        out_specs=[ON_CHIP] * len(outs),
        scratch_shapes=list(scratch),
        compiler_params=pltpu.CompilerParams(vmem_limit_bytes=SCOPED_BYTES),
        name=name,
    )(*args)


def product(left, right):
    return jnp.dot(left, right, preferred_element_type=F32)


def first_solve(tree, sub_rhs, diag_inverse):
    rhs_count, depth = sub_rhs.shape[2:]
    cols = diag_inverse.shape[2]
    pieces = 3
    step = depth // pieces

    def body(tree_ref, rhs_hbm, inverse_hbm, out_ref, rhs, inverse, rhs_sem, inverse_sem):
        rhs_copy = pltpu.make_async_copy(rhs_hbm.at[tree_ref[0], 0], rhs, rhs_sem)
        rhs_copy.start()
        copies = []
        for piece in range(pieces):
            part = pl.ds(piece * step, step)
            copies.append(
                pltpu.make_async_copy(
                    inverse_hbm.at[0, part], inverse.at[part], inverse_sem.at[piece]
                )
            )
            copies[-1].start()
        rhs_copy.wait()
        total = jnp.zeros((rhs_count, cols), F32)
        for piece in range(pieces):
            copies[piece].wait()
            part = slice(piece * step, (piece + 1) * step)
            total = total + product(rhs[:, part].astype(BF16), inverse[part, :])
        out_ref[...] = total

    return call(
        body,
        [((rhs_count, cols), F32)],
        (tree, sub_rhs, diag_inverse),
        [SCALARS, IN_PLACE, IN_PLACE],
        [
            pltpu.VMEM((rhs_count, depth), F32),
            pltpu.VMEM((depth, cols), BF16),
            pltpu.SemaphoreType.DMA,
            pltpu.SemaphoreType.DMA((pieces,)),
        ],
        "first_solve",
    )[0]


def next_solve(place, part, rhs, sums, diag_inverse):
    few = sums[0].shape[0]
    rows = slice(part * few, (part + 1) * few)

    def body(rhs_ref, *refs):
        *sum_refs, inverse_ref, out_ref = refs
        update = sum_refs[0][...]
        for ref in sum_refs[1:]:
            update = update + ref[...]
        residual = (rhs_ref[place, rows] - update).astype(BF16)
        out_ref[...] = product(residual, inverse_ref[place])

    shape = (few, diag_inverse.shape[2])
    return call(body, [(shape, F32)], (rhs, *sums, diag_inverse), name="next_solve")[0]


def mask_tiles(mask_ref, block, source, target):
    rows, cols = source.shape[1:]
    for i in range(rows // TILE):
        for j in range(cols // TILE):
            there = (
                block,
                slice(i * TILE, (i + 1) * TILE),
                slice(j * TILE, (j + 1) * TILE),
            )
            keep = jnp.full((TILE, TILE), mask_ref[block, i, j], F32).astype(BF16)
            target[there] = source[there] * keep


def stage(tree, mask, sub_rhs, diag_inverse, factor):
    levels, rhs_count, depth = sub_rhs.shape[1:]
    later = levels - 1
    cols = diag_inverse.shape[2]

    def body(
        tree_ref, mask_ref, rhs_hbm, inverse_hbm, factor_hbm, out_ref, inverse_ref, rhs_ref, landed, sems, other_sems
    ):
        blocks = factor_hbm.shape[0]
        copies = [
            pltpu.make_async_copy(factor_hbm.at[block], landed.at[block], sems.at[block])
            for block in range(blocks)
        ]
        others = [
            pltpu.make_async_copy(inverse_hbm.at[pl.ds(1, later)], inverse_ref, other_sems.at[0]),
            pltpu.make_async_copy(
                rhs_hbm.at[tree_ref[0], pl.ds(1, later)], rhs_ref, other_sems.at[1]
            ),
        ]
        for copy in copies + others:
            copy.start()
        for block, copy in enumerate(copies):
            copy.wait()
            mask_tiles(mask_ref, block, landed, out_ref)
        for copy in others:
            copy.wait()

    return call(
        body,
        [
            (factor.shape, BF16),
            ((later, depth, cols), BF16),
            ((later, rhs_count, depth), F32),
        ],
        (tree, mask, sub_rhs, diag_inverse, factor),
        [SCALARS, SCALARS, IN_PLACE, IN_PLACE, IN_PLACE],
        [
            pltpu.VMEM(factor.shape, BF16),
            pltpu.SemaphoreType.DMA((factor.shape[0],)),
            pltpu.SemaphoreType.DMA((2,)),
        ],
        "stage",
    )


def masked(mask, factor):
    def body(mask_ref, factor_ref, out_ref):
        for block in range(factor.shape[0]):
            mask_tiles(mask_ref, block, factor_ref, out_ref)

    return call(
        body, [(factor.shape, BF16)], (mask, factor), [SCALARS, ON_CHIP], name="masked"
    )[0]


def stacked(parts):
    levels, count = len(parts), len(parts[0])
    rows, cols = parts[0][0].shape

    def body(*refs):
        *part_refs, out_hbm, sems = refs
        copies = [
            pltpu.make_async_copy(
                ref, out_hbm.at[k // count, pl.ds(k % count * rows, rows)], sems.at[k]
            )
            for k, ref in enumerate(part_refs)
        ]
        for copy in copies:
            copy.start()
        for copy in copies:
            copy.wait()

    args = [pltpu.with_memory_space_constraint(part, pltpu.VMEM) for one in parts for part in one]
    return pl.pallas_call(
        body,
        out_shape=jax.ShapeDtypeStruct((levels, count * rows, cols), F32),
        in_specs=[ON_CHIP] * len(args),
        out_specs=IN_PLACE,
        scratch_shapes=[pltpu.SemaphoreType.DMA((len(args),))],
        compiler_params=pltpu.CompilerParams(vmem_limit_bytes=SCOPED_BYTES),
        name="stacked",
    )(*args)


def kept_update(halves, factor, block, before, parts=1, last=False):
    rows, cols = halves[0].shape
    out_cols = factor.shape[2]
    few = rows // parts
    places = [slice(k * few, (k + 1) * few) for k in range(parts)]

    def body(one_ref, other_ref, factor_ref, *refs):
        before_refs, outs = refs[: len(before)], refs[len(before) :]
        solved = one_ref[...] + other_ref[...]
        kept = solved.astype(BF16)
        update = product(kept, factor_ref[block])
        for ref in before_refs:
            update = update + ref[...]
        for k, whole in enumerate((update, solved, kept)):
            for ref, place in zip(outs[k * parts : (k + 1) * parts], places):
                ref[...] = whole[place]

    kinds = [((few, out_cols), F32), ((few, cols), F32), ((few, cols), BF16)]
    outs = [kind for kind in kinds[: 2 if last else 3] for _ in range(parts)]
    return call(body, outs, (*halves, factor, *before), name="kept_update")


def early_update(kept, factor, blocks):
    def body(*refs):
        *kept_refs, factor_ref, out_ref = refs
        update = product(kept_refs[0][...], factor_ref[blocks[0]])
        for ref, block in zip(kept_refs[1:], blocks[1:]):
            update = update + product(ref[...], factor_ref[block])
        out_ref[...] = update

    shape = (kept[0].shape[0], factor.shape[2])
    return call(body, [(shape, F32)], (*kept, factor), name="early_update")[0]


def root_part(rhs_rows, update_parts, root_inverse):
    def body(rhs_ref, one_ref, other_ref, inverse_ref, out_ref):
        residual = rhs_ref[...] - (one_ref[...] + other_ref[...])
        out_ref[...] = product(residual.astype(BF16), inverse_ref[...])

    shape = (rhs_rows.shape[0], root_inverse.shape[1])
    return call(
        body, [(shape, F32)], (rhs_rows, *update_parts, root_inverse), name="root_part"
    )[0]


def prow_halves(partial_sum, part=0):
    near, far = ("core", "xl") if part % 2 == 0 else ("xl", "core")
    pair = partial_sum + partner(partial_sum, near)
    return pair, partner(pair, far)


def owner_sums(partial_sum, part):
    if part % 2 == 0:
        pair = partial_sum + partner(partial_sum, OWN, 4)
        return [pair] + [partner(pair, OWN, bit) for bit in (2, 3, 1)]
    far, back, near = [partner(partial_sum, OWN, bit) for bit in (2, 3, 1)]
    line = (partial_sum + near) + (far + back)
    return [line, partner(line, OWN, 4)]


def shards(
    sub_rhs, root_rhs, diag_inverse, root_inverse, inner_factor, inner_mask, root_factor, root_mask
):
    out_cols = inner_factor.shape[2]
    rhs_count = root_rhs.shape[0]
    tiles = out_cols // TILE
    tree = lax.axis_index("zt")
    first_tile = lax.axis_index(PROW) * tiles
    inner_tiles = lax.dynamic_slice_in_dim(inner_mask, first_tile, tiles, 2)
    root_tiles = lax.dynamic_slice_in_dim(root_mask, first_tile, tiles, 2)
    tree = tree.reshape(1)

    halves = prow_halves(first_solve(tree, sub_rhs, diag_inverse))
    inner, inverse, rhs = stage(tree, inner_tiles, sub_rhs, diag_inverse, inner_factor)
    root = masked(root_tiles, root_factor)
    solved, locals_ = [], []
    outs = kept_update(halves, inner, 0, (), PARTS)
    for part in range(PARTS):
        update, solved0, kept0 = outs[part::PARTS]
        halves = prow_halves(next_solve(0, part, rhs, owner_sums(update, part), inverse), part)
        early = early_update((kept0,), inner, (1,))
        update, solved1, kept1 = kept_update(halves, inner, 2, (early,))
        early = early_update((kept0, kept1), root, (0, 1))
        *sums, early = lax.optimization_barrier((*owner_sums(update, part), early))
        halves = prow_halves(next_solve(1, part, rhs, sums, inverse), part)
        root_local, solved2 = kept_update(halves, root, 2, (early,), last=True)
        solved.append((solved0, solved1, solved2))
        locals_.append(root_local)
    root_local = jnp.concatenate(locals_)

    owners = lax.axis_size(OWN)
    few = rhs_count // owners
    place = owners - 1 - lax.axis_index(OWN)
    own_rows = swap_blocks(root_local.reshape(owners, few, out_cols)).sum(axis=0)
    sub_solution, across = lax.optimization_barrier(
        (stacked(list(zip(*solved))), partner(own_rows, "grid"))
    )
    total = own_rows + across
    total = total + partner(total, "zt", 1)
    rhs_rows = lax.dynamic_slice_in_dim(root_rhs, place * few, few, 0)
    part = root_part(rhs_rows, (total, partner(total, "zt", 3)), root_inverse)
    pair, other = prow_halves(part)
    root_solution = to_everyone(pair + other).reshape(rhs_count, part.shape[1])
    return (sub_solution, root_solution)


def solution(mesh):
    prow, pcol = mesh.shape["prow"], mesh.shape["pcol"]
    cores = 2
    trees = 8 // mesh.shape["grid"]
    fine = Mesh(
        mesh.devices.reshape(
            mesh.shape["grid"], prow // cores, cores, trees, pcol // trees
        ),
        ("grid", "xl", "core", "zt", "own"),
    )
    columns = ("grid", "zt", "own")
    return jax.shard_map(
        shards,
        mesh=fine,
        in_specs=(
            P("grid", None, None, PROW),
            P(None, PROW),
            P(None, PROW, columns),
            P(PROW, "grid"),
            P(None, columns, PROW),
            P(None, columns, None),
            P(None, columns, PROW),
            P(None, columns, None),
        ),
        out_specs=(P(None, None, columns), P(None, "grid")),
        check_vma=False,
    )
```

```python
import jax
import jax.numpy as jnp
from jax import lax
from jax.experimental import pallas as pl
from jax.experimental.pallas import tpu as pltpu
from jax.sharding import Mesh
from jax.sharding import PartitionSpec as P

LEVELS = 3
TILE = 128
PARTS = 2
PROW = ("xl", "core")
OWN = "own"
SCOPED_BYTES = 4 << 20
F32 = jnp.float32
BF16 = jnp.bfloat16

ON_CHIP = pl.BlockSpec(memory_space=pltpu.VMEM)
SCALARS = pl.BlockSpec(memory_space=pltpu.SMEM)
IN_PLACE = pl.BlockSpec(memory_space=pltpu.HBM)


def partner(shard, axis, bit=1):
    return lax.ppermute(shard, axis, [(i, i ^ bit) for i in range(lax.axis_size(axis))])


def swap_blocks(blocks):
    order = list(range(lax.axis_size(OWN)))[::-1]
    return lax.all_to_all(blocks, OWN, 0, 0, axis_index_groups=[order], tiled=True)


def to_everyone(shard):
    count = lax.axis_size(OWN)
    return swap_blocks(jnp.broadcast_to(shard[None], (count, *shard.shape)))


def call(body, outs, args, specs=None, scratch=(), name=None):
    specs = specs or [ON_CHIP] * len(args)
    args = [
        arg if spec is SCALARS else pltpu.with_memory_space_constraint(arg, spec.memory_space)
        for arg, spec in zip(args, specs)
    ]
    return pl.pallas_call(
        body,
        out_shape=[pltpu.VMEM(shape, kind) for shape, kind in outs],
        in_specs=specs,
        out_specs=[ON_CHIP] * len(outs),
        scratch_shapes=list(scratch),
        compiler_params=pltpu.CompilerParams(vmem_limit_bytes=SCOPED_BYTES),
        name=name,
    )(*args)


def product(left, right):
    return jnp.dot(left, right, preferred_element_type=F32)


def first_solve(tree, sub_rhs, diag_inverse):
    rhs_count, depth = sub_rhs.shape[2:]
    cols = diag_inverse.shape[2]
    pieces = 3
    step = depth // pieces

    def body(tree_ref, rhs_hbm, inverse_hbm, out_ref, rhs, inverse, rhs_sem, inverse_sem):
        rhs_copy = pltpu.make_async_copy(rhs_hbm.at[tree_ref[0], 0], rhs, rhs_sem)
        rhs_copy.start()
        copies = []
        for piece in range(pieces):
            part = pl.ds(piece * step, step)
            copies.append(
                pltpu.make_async_copy(
                    inverse_hbm.at[0, part], inverse.at[part], inverse_sem.at[piece]
                )
            )
            copies[-1].start()
        rhs_copy.wait()
        total = jnp.zeros((rhs_count, cols), F32)
        for piece in range(pieces):
            copies[piece].wait()
            part = slice(piece * step, (piece + 1) * step)
            total = total + product(rhs[:, part].astype(BF16), inverse[part, :])
        out_ref[...] = total

    return call(
        body,
        [((rhs_count, cols), F32)],
        (tree, sub_rhs, diag_inverse),
        [SCALARS, IN_PLACE, IN_PLACE],
        [
            pltpu.VMEM((rhs_count, depth), F32),
            pltpu.VMEM((depth, cols), BF16),
            pltpu.SemaphoreType.DMA,
            pltpu.SemaphoreType.DMA((pieces,)),
        ],
        "first_solve",
    )[0]


def next_solve(place, part, rhs, sums, diag_inverse):
    few = sums[0].shape[0]
    rows = slice(part * few, (part + 1) * few)

    def body(rhs_ref, *refs):
        *sum_refs, inverse_ref, out_ref = refs
        update = sum_refs[0][...]
        for ref in sum_refs[1:]:
            update = update + ref[...]
        residual = (rhs_ref[place, rows] - update).astype(BF16)
        out_ref[...] = product(residual, inverse_ref[place])

    shape = (few, diag_inverse.shape[2])
    return call(body, [(shape, F32)], (rhs, *sums, diag_inverse), name="next_solve")[0]


def mask_tiles(mask_ref, block, source, target):
    rows, cols = source.shape[1:]
    for i in range(rows // TILE):
        for j in range(cols // TILE):
            there = (
                block,
                slice(i * TILE, (i + 1) * TILE),
                slice(j * TILE, (j + 1) * TILE),
            )
            keep = jnp.full((TILE, TILE), mask_ref[block, i, j], F32).astype(BF16)
            target[there] = source[there] * keep


def stage(tree, mask, sub_rhs, diag_inverse, factor):
    levels, rhs_count, depth = sub_rhs.shape[1:]
    later = levels - 1
    cols = diag_inverse.shape[2]

    def body(
        tree_ref, mask_ref, rhs_hbm, inverse_hbm, factor_hbm, out_ref, inverse_ref, rhs_ref, landed, sems, other_sems
    ):
        blocks = factor_hbm.shape[0]
        copies = [
            pltpu.make_async_copy(factor_hbm.at[block], landed.at[block], sems.at[block])
            for block in range(blocks)
        ]
        others = [
            pltpu.make_async_copy(inverse_hbm.at[pl.ds(1, later)], inverse_ref, other_sems.at[0]),
            pltpu.make_async_copy(
                rhs_hbm.at[tree_ref[0], pl.ds(1, later)], rhs_ref, other_sems.at[1]
            ),
        ]
        for copy in copies + others:
            copy.start()
        for block, copy in enumerate(copies):
            copy.wait()
            mask_tiles(mask_ref, block, landed, out_ref)
        for copy in others:
            copy.wait()

    return call(
        body,
        [
            (factor.shape, BF16),
            ((later, depth, cols), BF16),
            ((later, rhs_count, depth), F32),
        ],
        (tree, mask, sub_rhs, diag_inverse, factor),
        [SCALARS, SCALARS, IN_PLACE, IN_PLACE, IN_PLACE],
        [
            pltpu.VMEM(factor.shape, BF16),
            pltpu.SemaphoreType.DMA((factor.shape[0],)),
            pltpu.SemaphoreType.DMA((2,)),
        ],
        "stage",
    )


def masked(mask, factor):
    def body(mask_ref, factor_ref, out_ref):
        for block in range(factor.shape[0]):
            mask_tiles(mask_ref, block, factor_ref, out_ref)

    return call(
        body, [(factor.shape, BF16)], (mask, factor), [SCALARS, ON_CHIP], name="masked"
    )[0]


def stacked(parts):
    levels, count = len(parts), len(parts[0])
    rows, cols = parts[0][0].shape

    def body(*refs):
        *part_refs, out_hbm, sems = refs
        copies = [
            pltpu.make_async_copy(
                ref, out_hbm.at[k // count, pl.ds(k % count * rows, rows)], sems.at[k]
            )
            for k, ref in enumerate(part_refs)
        ]
        for copy in copies:
            copy.start()
        for copy in copies:
            copy.wait()

    args = [pltpu.with_memory_space_constraint(part, pltpu.VMEM) for one in parts for part in one]
    return pl.pallas_call(
        body,
        out_shape=jax.ShapeDtypeStruct((levels, count * rows, cols), F32),
        in_specs=[ON_CHIP] * len(args),
        out_specs=IN_PLACE,
        scratch_shapes=[pltpu.SemaphoreType.DMA((len(args),))],
        compiler_params=pltpu.CompilerParams(vmem_limit_bytes=SCOPED_BYTES),
        name="stacked",
    )(*args)


def kept_update(halves, factor, block, before, parts=1, last=False):
    rows, cols = halves[0].shape
    out_cols = factor.shape[2]
    few = rows // parts
    places = [slice(k * few, (k + 1) * few) for k in range(parts)]

    def body(one_ref, other_ref, factor_ref, *refs):
        before_refs, outs = refs[: len(before)], refs[len(before) :]
        solved = one_ref[...] + other_ref[...]
        kept = solved.astype(BF16)
        update = product(kept, factor_ref[block])
        for ref in before_refs:
            update = update + ref[...]
        for k, whole in enumerate((update, solved, kept)):
            for ref, place in zip(outs[k * parts : (k + 1) * parts], places):
                ref[...] = whole[place]

    kinds = [((few, out_cols), F32), ((few, cols), F32), ((few, cols), BF16)]
    outs = [kind for kind in kinds[: 2 if last else 3] for _ in range(parts)]
    return call(body, outs, (*halves, factor, *before), name="kept_update")


def early_update(kept, factor, blocks):
    def body(*refs):
        *kept_refs, factor_ref, out_ref = refs
        update = product(kept_refs[0][...], factor_ref[blocks[0]])
        for ref, block in zip(kept_refs[1:], blocks[1:]):
            update = update + product(ref[...], factor_ref[block])
        out_ref[...] = update

    shape = (kept[0].shape[0], factor.shape[2])
    return call(body, [(shape, F32)], (*kept, factor), name="early_update")[0]


def root_part(rhs_rows, update_parts, root_inverse):
    def body(rhs_ref, one_ref, other_ref, inverse_ref, out_ref):
        residual = rhs_ref[...] - (one_ref[...] + other_ref[...])
        out_ref[...] = product(residual.astype(BF16), inverse_ref[...])

    shape = (rhs_rows.shape[0], root_inverse.shape[1])
    return call(
        body, [(shape, F32)], (rhs_rows, *update_parts, root_inverse), name="root_part"
    )[0]


def prow_halves(partial_sum):
    pair = partial_sum + partner(partial_sum, "core")
    return pair, partner(pair, "xl")


def owner_sums(partial_sum, part):
    if part % 2 == 0:
        pair = partial_sum + partner(partial_sum, OWN, 4)
        return [pair] + [partner(pair, OWN, bit) for bit in (2, 3, 1)]
    far, back, near = [partner(partial_sum, OWN, bit) for bit in (2, 3, 1)]
    line = (partial_sum + near) + (far + back)
    return [line, partner(line, OWN, 4)]


def shards(
    sub_rhs, root_rhs, diag_inverse, root_inverse, inner_factor, inner_mask, root_factor, root_mask
):
    out_cols = inner_factor.shape[2]
    rhs_count = root_rhs.shape[0]
    tiles = out_cols // TILE
    tree = lax.axis_index("zt")
    first_tile = lax.axis_index(PROW) * tiles
    inner_tiles = lax.dynamic_slice_in_dim(inner_mask, first_tile, tiles, 2)
    root_tiles = lax.dynamic_slice_in_dim(root_mask, first_tile, tiles, 2)
    tree = tree.reshape(1)

    halves = prow_halves(first_solve(tree, sub_rhs, diag_inverse))
    inner, inverse, rhs = stage(tree, inner_tiles, sub_rhs, diag_inverse, inner_factor)
    root = masked(root_tiles, root_factor)
    solved, locals_ = [], []
    outs = kept_update(halves, inner, 0, (), PARTS)
    for part in range(PARTS):
        update, solved0, kept0 = outs[part::PARTS]
        halves = prow_halves(next_solve(0, part, rhs, owner_sums(update, part), inverse))
        early = early_update((kept0,), inner, (1,))
        update, solved1, kept1 = kept_update(halves, inner, 2, (early,))
        early = early_update((kept0, kept1), root, (0, 1))
        *sums, early = lax.optimization_barrier((*owner_sums(update, part), early))
        halves = prow_halves(next_solve(1, part, rhs, sums, inverse))
        root_local, solved2 = kept_update(halves, root, 2, (early,), last=True)
        solved.append((solved0, solved1, solved2))
        locals_.append(root_local)
    root_local = jnp.concatenate(locals_)

    owners = lax.axis_size(OWN)
    few = rhs_count // owners
    place = owners - 1 - lax.axis_index(OWN)
    own_rows = swap_blocks(root_local.reshape(owners, few, out_cols)).sum(axis=0)
    sub_solution, across = lax.optimization_barrier(
        (stacked(list(zip(*solved))), partner(own_rows, "grid"))
    )
    total = own_rows + across
    total = total + partner(total, "zt", 1)
    rhs_rows = lax.dynamic_slice_in_dim(root_rhs, place * few, few, 0)
    part = root_part(rhs_rows, (total, partner(total, "zt", 3)), root_inverse)
    pair, other = prow_halves(part)
    root_solution = to_everyone(pair + other).reshape(rhs_count, part.shape[1])
    return (sub_solution, root_solution)


def solution(mesh):
    prow, pcol = mesh.shape["prow"], mesh.shape["pcol"]
    cores = 2
    trees = 8 // mesh.shape["grid"]
    fine = Mesh(
        mesh.devices.reshape(
            mesh.shape["grid"], prow // cores, cores, trees, pcol // trees
        ),
        ("grid", "xl", "core", "zt", "own"),
    )
    columns = ("grid", "zt", "own")
    return jax.shard_map(
        shards,
        mesh=fine,
        in_specs=(
            P("grid", None, None, PROW),
            P(None, PROW),
            P(None, PROW, columns),
            P(PROW, "grid"),
            P(None, columns, PROW),
            P(None, columns, None),
            P(None, columns, PROW),
            P(None, columns, None),
        ),
        out_specs=(P(None, None, columns), P(None, "grid")),
        check_vma=False,
    )
```
